512 devices in a mesh: band: 32 (over z_hi, x, core), chan: 16 (over y, z_lo).
Axes of the slice: x: 4, y: 8, z: 8 (z_hi: 4, z_lo: 2; z = z_hi * 2 + z_lo), core: 2. Of those that a mesh axis runs over, the one named last changes fastest.
Arguments:
- image: bfloat16 [512, 128, 512], P('chan', 'band'), may hold values from -6 to 6
- filters: bfloat16 [9, 512, 512], P(None, None, 'chan'), may hold values from -0.09375 to 0.09375
- bias: bfloat16 [512], P('chan'), may hold values from -3 to 3
- upstream: bfloat16 [512, 128, 512], P('chan', 'band'), may hold values from -6 to 6
Outputs:
- features: bfloat16 [512, 128, 512], P('chan', 'band')
- image_grad: bfloat16 [512, 128, 512], P('chan', 'band')
The draws below stay inside these ranges and needn't reach their ends.
All inputs are finite; a program needn't handle non-finite values.
Results may differ from the reference program's by a relative error of at most 0.001.
Values may be sent and summed in bfloat16 or wider, within the bound.
A program may use at most 64 MiB of HBM per device.

```python
import jax
import jax.numpy as jnp
from jax import lax

CH = 512
COLS = 512
ROWS = 128


def levels(stream_key, extent, cuts, smallest, top_value):
    def one(position, parts):
        draws = jax.random.uniform(jax.random.fold_in(jax.random.fold_in(stream_key, 6), position), (parts,), jnp.float32, smallest / len(cuts), top_value / len(cuts))
        return jnp.repeat(jnp.exp(draws), extent[position] // parts).reshape((-1,) + (1,) * (len(extent) - position - 1))

    gain = one(*cuts[0])
    for cut in cuts[1:]:
        gain = gain * one(*cut)
    return gain


def noise(own_key, dims, deviation, bound, pieces=(), kind=jnp.bfloat16):
    factor_of = levels(own_key, dims, pieces, -0.22, 0.18) if pieces else 1.0
    array = jax.random.normal(own_key, dims, jnp.float32) * deviation * factor_of
    return jnp.minimum(jnp.maximum(array, -bound), bound).astype(kind)


def setup_inputs(seed: int = 0) -> dict:
    key_of = jax.random.split(jax.random.key(seed), 5)
    return {
        "image": noise(key_of[0], (CH, ROWS, COLS), 1.0, 6.0, ((0, 16), (1, 32))),
        "filters": noise(key_of[1], (9, CH, CH), (9 * CH) ** -0.5, 0.09375, ((2, 16),)),
        "bias": noise(key_of[2], (CH,), 0.5, 3.0, ((0, 16),)),
        "upstream": noise(key_of[3], (CH, ROWS, COLS), 1.0, 6.0, ((0, 16), (1, 32))),
    }


def reference(image, filters, bias, upstream):
    image_pad = jnp.pad(image.astype(jnp.float32), ((0, 0), (1, 1), (1, 1)))
    upstream_pad = jnp.pad(upstream.astype(jnp.float32), ((0, 0), (1, 1), (1, 1)))
    weights = filters.astype(jnp.float32)
    forward_acc = jnp.zeros((CH, ROWS, COLS), jnp.float32)
    backward_acc = jnp.zeros((CH, ROWS, COLS), jnp.float32)
    for tap_row in range(3):
        for tap_col in range(3):
            tap_index = tap_row * 3 + tap_col
            forward_acc = forward_acc + jnp.einsum(
                "oi,irc->orc", weights[tap_index],
                image_pad[:, tap_row:tap_row + ROWS, tap_col:tap_col + COLS],
                precision=lax.Precision.HIGHEST)
            backward_acc = backward_acc + jnp.einsum(
                "oi,orc->irc", weights[tap_index],
                upstream_pad[:, 2 - tap_row:2 - tap_row + ROWS, 2 - tap_col:2 - tap_col + COLS],
                precision=lax.Precision.HIGHEST)
    features = (forward_acc + bias.astype(jnp.float32)[:, None, None]).astype(jnp.bfloat16)
    image_grad = backward_acc.astype(jnp.bfloat16)
    return features, image_grad
```

```python
import jax
import jax.numpy as jnp
from jax import lax
from jax.experimental import pallas as pl
from jax.experimental.pallas import tpu as pltpu
from jax.sharding import PartitionSpec as P

MESH = pl.DeviceIdType.MESH
BF16, F32 = jnp.bfloat16, jnp.float32


def kernel(keep, give, filt, bias, mine, other, gathered, weights, packed, pieces,
           products, rim_out, rim_in, bias_in, staged,
           ring_send, ring_recv, pair_send, pair_recv, piece_send, piece_recv,
           share_send, rim_send, rim_recv, out_send, out_recv):
    band, chan = lax.axis_index("band"), lax.axis_index("chan")
    core, x, z_hi = band % 2, (band // 2) % 4, band // 8
    y, z_lo = chan // 2, chan % 2
    partner = {"band": band, "chan": chan + 1 - 2 * z_lo}
    up_ring = {"band": band, "chan": (chan + 2) % 16}
    down_ring = {"band": band, "chan": (chan + 14) % 16}
    above = {"band": (band + 31) % 32, "chan": chan}
    below = {"band": (band + 1) % 32, "chan": chan}

    def same_place(k):
        other_x, other_core = (x + k // 2) % 4, (core + k % 2) % 2
        return {"band": z_hi * 8 + other_x * 2 + other_core, "chan": chan}

    def same_band(k):
        return {"band": band, "chan": (chan + k) % 16}

    barrier = pltpu.get_barrier_semaphore()
    peers = [same_band(k) for k in range(1, 16)] + [same_place(k) for k in range(1, 8)]
    for peer in peers + [above, below]:
        pl.semaphore_signal(barrier, inc=1, device_id=peer, device_id_type=MESH)
    pl.semaphore_wait(barrier, len(peers) + 2)

    def remote(src, dst, send, recv, where):
        return pltpu.make_async_remote_copy(
            src_ref=src, dst_ref=dst, send_sem=send, recv_sem=recv,
            device_id=where, device_id_type=MESH)

    partner_chan = chan + 1 - 2 * z_lo
    started = []

    def ring(direction, hop, src, owner):
        copy = remote(src, gathered.at[:, owner], ring_send.at[direction, hop],
                      ring_recv.at[direction, hop], up_ring if direction == 0 else down_ring)
        copy.start()
        started.append(copy)

    pair = remote(give, gathered.at[:, chan], pair_send.at[0], pair_recv.at[0], partner)
    pair.start()
    ring(0, 0, keep, chan)
    ring(1, 0, keep, chan)
    biases = remote(bias, bias_in, pair_send.at[1], pair_recv.at[1], partner)
    biases.start()

    @pl.when((core == z_lo) & (x == y % 4))
    def _():
        lane = lax.broadcasted_iota(jnp.int32, (32, 128), 1)
        for q in range(4):
            for j in range(5):
                a = filt[2 * j, :, 128 * q : 128 * q + 128].astype(F32)
                b = filt[2 * j + 1, :, 128 * q : 128 * q + 128].astype(F32) if j < 4 else a
                packed[2 * q, j] = jnp.where(lane < 64, a, pltpu.roll(b, 64, 1)).astype(BF16)
                packed[2 * q + 1, j] = jnp.where(lane < 64, pltpu.roll(a, 64, 1), b).astype(BF16)
        for d in range(1, 8):
            remote(packed.at[(y + d) % 8], pieces.at[:, chan], piece_send.at[d],
                   piece_recv.at[chan], {"band": band, "chan": 2 * ((y + d) % 8)}).start()

        @pl.when(z_lo == 0)
        def _():
            pltpu.make_async_copy(packed.at[y], pieces.at[:, chan], piece_recv.at[chan]).start()

        @pl.when(z_lo == 1)
        def _():
            remote(packed.at[y], pieces.at[:, chan], piece_send.at[0],
                   piece_recv.at[chan], partner).start()

    gradient_filters = remote(filt, weights.at[0:9, 0:32], pair_send.at[2], pair_recv.at[2], partner)

    @pl.when(z_lo == 0)
    def _():
        gradient_filters.start()

    @pl.when(z_lo == 1)
    def _():
        weights[0:9, 32:64] = filt[...]

    gathered[:, chan] = keep[...]

    def piece_wait(owner):
        remote(packed.at[0], pieces.at[:, owner], piece_send.at[0], piece_recv.at[owner], partner).wait_recv()

    def ring_wait(direction, hop, owner):
        remote(keep, gathered.at[:, owner], ring_send.at[direction, hop],
               ring_recv.at[direction, hop], partner).wait_recv()

    pair.wait_recv()
    ring(0, 1, gathered.at[:, partner_chan], partner_chan)
    ring(1, 1, gathered.at[:, partner_chan], partner_chan)

    def owner_of(direction, hop):
        away = hop // 2 + 1
        base = (chan + 16 - 2 * away) % 16 if direction == 0 else (chan + 2 * away) % 16
        if hop == 6:
            return base if direction == 0 else base + 1 - 2 * z_lo
        return base if hop % 2 == 0 else base + 1 - 2 * z_lo

    for hop in range(7):
        for direction in range(2):
            owner = owner_of(direction, hop)
            ring_wait(direction, hop, owner)
            if hop + 2 < 6 or (hop + 2 == 6 and direction == 0):
                ring(direction, hop + 2, gathered.at[:, owner], owner)
            if hop == 5 and direction == 1:
                ring(1, 6, gathered.at[:, owner], owner)
        if hop == 1:
            @pl.when(z_lo == 0)
            def _():
                for m in range(2):
                    owner = 2 * (x + 4 * m) + core
                    piece_wait(owner)
                    for k in range(1, 8):
                        remote(pieces.at[:, owner], pieces.at[:, owner], share_send.at[m, k],
                               piece_recv.at[owner], same_place(k)).start()
        if hop == 4:
            @pl.when(z_lo == 0)
            def _():
                for k in range(1, 8):
                    band_of = same_place(k)["band"]
                    for m in range(2):
                        piece_wait(2 * ((band_of // 2) % 4 + 4 * m) + band_of % 2)
                for j in range(5):
                    weights[2 * j : 2 * j + 2] = pieces[j].reshape(512, 128).T.reshape(2, 64, 512)

            @pl.when(z_lo == 1)
            def _():
                gradient_filters.wait_recv()

    lhs = weights[0:9].reshape(576, 512)

    def multiply(q, carry):
        for half in range(2):
            columns = slice(256 * half, 256 * half + 256)
            rhs = gathered[q, :, :, columns].reshape(512, 256)
            products[q, :, :, columns] = jnp.dot(
                lhs, rhs, preferred_element_type=F32).reshape(9, 64, 256)
        return carry

    lax.fori_loop(0, 4, multiply, 0)

    column = lax.broadcasted_iota(jnp.int32, (64, 512), 1)

    def tap(a, b):
        return 3 * a + b + z_lo * (8 - 2 * (3 * a + b))

    def row_sum(terms):
        left, mid, right = [sum(products[q, tap(a, b)] for q, a in terms) for b in range(3)]
        left = jnp.where(column == 0, 0.0, pltpu.roll(left, 1, 1))
        right = jnp.where(column == 511, 0.0, pltpu.roll(right, 511, 1))
        return left + mid + right

    rim_out[0] = row_sum([(0, 2)])
    to_above = remote(rim_out.at[0], rim_in.at[0], rim_send.at[0], rim_recv.at[0], above)
    to_above.start()
    rim_out[1] = row_sum([(3, 0)])
    to_below = remote(rim_out.at[1], rim_in.at[1], rim_send.at[1], rim_recv.at[1], below)
    to_below.start()

    biases.wait_recv()
    own_bias, partner_bias = bias[:, 0:1], bias_in[:, 0:1]
    offset = jnp.concatenate([own_bias, partner_bias], axis=0)
    offset = jnp.where(z_lo == 0, offset, jnp.zeros_like(offset))
    outgoing = []
    for r in (1, 2, 0, 3):
        total = row_sum([(r + a - 1, a) for a in range(3) if 0 <= r + a - 1 < 4])
        if r == 0:
            to_below.wait_recv()
            total = total + jnp.where(band > 0, rim_in[1], 0.0)
        if r == 3:
            to_above.wait_recv()
            total = total + jnp.where(band < 31, rim_in[0], 0.0)
        total = (total + offset).astype(BF16)
        low, high = total[0:32], total[32:64]
        mine[r] = jnp.where(z_lo == 0, low, high)
        staged[r] = jnp.where(z_lo == 0, high, low)
        copy = remote(staged.at[r], other.at[r], out_send.at[r], out_recv.at[r], partner)
        copy.start()
        outgoing.append(copy)

    for copy in started:
        copy.wait_send()
    pair.wait_send()
    biases.wait_send()
    to_above.wait_send()
    to_below.wait_send()

    @pl.when((core == z_lo) & (x == y % 4))
    def _():
        for d in range(1, 8):
            remote(packed.at[0], pieces.at[:, 0], piece_send.at[d], piece_recv.at[0], partner).wait_send()

        @pl.when(z_lo == 1)
        def _():
            remote(packed.at[0], pieces.at[:, 0], piece_send.at[0], piece_recv.at[0], partner).wait_send()

    @pl.when(z_lo == 0)
    def _():
        gradient_filters.wait_send()
        for m in range(2):
            for k in range(1, 8):
                remote(pieces.at[:, 0], pieces.at[:, 0], share_send.at[m, k], piece_recv.at[0], partner).wait_send()

    for copy in outgoing:
        copy.wait()


def per_device(image, filters, bias, upstream):
    forward = lax.axis_index("chan") % 2 == 0
    rows_first = [jnp.transpose(value, (1, 0, 2)) for value in (image, upstream)]
    keep = jnp.where(forward, *rows_first)
    give = jnp.where(forward, *rows_first[::-1])
    filt = jnp.transpose(filters, (0, 2, 1))
    wide_bias = jnp.broadcast_to(bias.astype(F32)[:, None], (32, 128))
    block = jax.ShapeDtypeStruct((4, 32, 512), BF16)
    vmem = pl.BlockSpec(memory_space=pltpu.VMEM)
    dma = pltpu.SemaphoreType.DMA
    mine, other = pl.pallas_call(
        kernel,
        out_shape=(block, block),
        in_specs=[vmem] * 4,
        out_specs=(vmem, vmem),
        scratch_shapes=[
            pltpu.VMEM((4, 16, 32, 512), BF16),
            pltpu.VMEM((10, 64, 512), BF16),
            pltpu.VMEM((8, 5, 32, 128), BF16),
            pltpu.VMEM((5, 16, 32, 128), BF16),
            pltpu.VMEM((4, 9, 64, 512), F32),
            pltpu.VMEM((2, 64, 512), F32),
            pltpu.VMEM((2, 64, 512), F32),
            pltpu.VMEM((32, 128), F32),
            pltpu.VMEM((4, 32, 512), BF16),
            dma((2, 7)), dma((2, 7)), dma((3,)), dma((3,)), dma((8,)), dma((16,)),
            dma((2, 8)), dma((2,)), dma((2,)), dma((4,)), dma((4,)),
        ],
        compiler_params=pltpu.CompilerParams(
            collective_id=0, has_side_effects=True, vmem_limit_bytes=40 << 20),
        name="conv_both",
    )(keep, give, filt, wide_bias)
    features = jnp.transpose(jnp.where(forward, mine, other), (1, 0, 2))
    image_grad = jnp.transpose(jnp.where(forward, other, mine), (1, 0, 2))
    return features, image_grad


def solution(mesh):
    return jax.shard_map(
        per_device,
        mesh=mesh,
        in_specs=(
            P("chan", "band", None),
            P(None, None, "chan"),
            P("chan"),
            P("chan", "band", None),
        ),
        out_specs=(P("chan", "band", None), P("chan", "band", None)),
        check_vma=False,
    )
```

```python
import jax
import jax.numpy as jnp
from jax import lax
from jax.experimental import pallas as pl
from jax.experimental.pallas import tpu as pltpu
from jax.sharding import PartitionSpec as P

MESH = pl.DeviceIdType.MESH
BF16, F32 = jnp.bfloat16, jnp.float32


def kernel(keep, give, filt, bias, mine, other, gathered, halo, weights, packed, pieces,
           products, halo_products, bias_own, bias_in, staged,
           ring_send, ring_recv, pair_send, pair_recv, halo_send, halo_recv,
           filter_send, filter_recv, relay_send, piece_send, piece_recv, share_send,
           out_send, out_recv):
    band, chan = lax.axis_index("band"), lax.axis_index("chan")
    core, x, z_hi = band % 2, (band // 2) % 4, band // 8
    y, z_lo = chan // 2, chan % 2
    partner_chan = chan + 1 - 2 * z_lo
    partner = {"band": band, "chan": partner_chan}
    ring_next = ({"band": band, "chan": (chan + 2) % 16}, {"band": band, "chan": (chan + 14) % 16})
    twin = {"band": band + 1 - 2 * core, "chan": chan}
    outer_ok = ((core == 0) & (band > 0)) | ((core == 1) & (band < 31))
    outer = {"band": (band + 31 + 2 * core) % 32, "chan": chan}
    sends_filters = (core == z_lo) & (x == y % 4)

    def same_place(k):
        other_x, other_core = (x + k // 2) % 4, (core + k % 2) % 2
        return {"band": z_hi * 8 + other_x * 2 + other_core, "chan": chan}

    def slot_at(owner, place):
        return (owner + 16 - 4 * (((place + 7) // 2) % 4)) % 16

    def slot_of(owner):
        return slot_at(owner, y)

    def remote(src, dst, send, recv, where):
        return pltpu.make_async_remote_copy(
            src_ref=src, dst_ref=dst, send_sem=send, recv_sem=recv,
            device_id=where, device_id_type=MESH)

    barrier = pltpu.get_barrier_semaphore()

    def greet(where):
        pl.semaphore_signal(barrier, inc=1, device_id=where, device_id_type=MESH)

    for where in (partner, *ring_next):
        greet(where)

    @pl.when(outer_ok)
    def _():
        greet(outer)

    greet(twin)

    @pl.when(z_lo == 0)
    def _():
        for m in range(2):
            source = 2 * (x + 4 * m) + core

            @pl.when(source != chan)
            def _():
                greet({"band": band, "chan": source})
        for k in range(1, 8):
            if k != 1:
                greet(same_place(k))

    targets = 4 + jnp.where(outer_ok, 1, 0) + jnp.where(z_lo == 0, 6, 0)
    targets = targets + jnp.where(sends_filters, 7 + z_lo, 0)
    pl.semaphore_wait(barrier, targets)

    first_row = (3 * core, 1 - core)
    row_count = (1, 3)

    def rows(part):
        return pl.ds(first_row[part], row_count[part])

    def ring(direction, hop, part, owner, src):
        place = (y + 1) % 8 if direction == 0 else (y + 7) % 8
        return remote(src, gathered.at[rows(part), slot_at(owner, place)],
                      ring_send.at[direction, hop, part], ring_recv.at[direction, hop, part],
                      ring_next[direction])

    def own_block(part, owner):
        return gathered.at[rows(part), slot_of(owner)]

    def halo_copy(side, owner, src):
        slot = slot_of(owner)
        return remote(src, halo.at[side, slot], halo_send.at[side, slot],
                      halo_recv.at[side, slot], twin if side else outer)

    def send_halo(part, owner, block):
        if part == 0:
            @pl.when(outer_ok)
            def _():
                halo_copy(0, owner, block(3 * core)).start()
        else:
            halo_copy(1, owner, block(3 - 3 * core)).start()

    def in_gathered(owner):
        return lambda row: gathered.at[row, slot_of(owner)]

    def in_keep(row):
        return keep.at[row]

    started = []

    def start(copy):
        copy.start()
        started.append(copy)

    pairs = [remote(give.at[rows(part)], gathered.at[rows(part), slot_of(chan)],
                    pair_send.at[part], pair_recv.at[part], partner) for part in range(2)]
    for part in range(2):
        start(pairs[part])
        for direction in range(2):
            start(ring(direction, 0, part, chan, keep.at[rows(part)]))
        send_halo(part, chan, in_keep)

    @pl.when(sends_filters)
    def _():
        lane = lax.broadcasted_iota(jnp.int32, (32, 128), 1)
        for q in range(4):
            for j in range(5):
                a = filt[2 * j, :, 128 * q : 128 * q + 128].astype(F32)
                b = filt[2 * j + 1, :, 128 * q : 128 * q + 128].astype(F32) if j < 4 else a
                packed[2 * q, j] = jnp.where(lane < 64, a, pltpu.roll(b, 64, 1)).astype(BF16)
                packed[2 * q + 1, j] = jnp.where(lane < 64, pltpu.roll(a, 64, 1), b).astype(BF16)
        for d in range(1, 8):
            place = (y + d) % 8
            slot = slot_at(chan, place)
            remote(packed.at[place], pieces.at[:, slot], piece_send.at[d],
                   piece_recv.at[slot], {"band": band, "chan": 2 * place}).start()
        slot = slot_of(chan)

        @pl.when(z_lo == 0)
        def _():
            pltpu.make_async_copy(packed.at[y], pieces.at[:, slot], piece_recv.at[slot]).start()

        @pl.when(z_lo == 1)
        def _():
            remote(packed.at[y], pieces.at[:, slot], piece_send.at[0],
                   piece_recv.at[slot], partner).start()

    turn = ((y + 7) // 2) % 4

    def lanes(j):
        return pl.ds(pl.multiple_of(128 * ((j + turn) % 4), 128), 128)

    def from_partner(j):
        column = pl.ds(pl.multiple_of(128 * (2 * core + j), 128), 128)
        return remote(filt.at[:, :, lanes(2 * core + j)], weights.at[0:9, 0:32, column],
                      filter_send.at[j], filter_recv.at[2 * core + j], partner)

    def hand_on(j):
        column = pl.ds(pl.multiple_of(128 * (2 * core + j), 128), 128)
        return remote(weights.at[0:9, 0:32, column], weights.at[0:9, 0:32, column],
                      relay_send.at[j], filter_recv.at[2 * core + j], twin)

    def filters_wait(j, place):
        remote(filt.at[:, :, 0:128], weights.at[0:9, 0:32, 0:128],
               relay_send.at[j], filter_recv.at[2 * place + j], twin).wait_recv()

    diagonal = (lax.broadcasted_iota(jnp.int32, (32, 32), 0)
                == lax.broadcasted_iota(jnp.int32, (32, 32), 1))
    spread = jnp.where(diagonal, jnp.broadcast_to(bias[...].astype(F32), (32, 32)), 0.0)
    bias_own[...] = jnp.broadcast_to(jnp.sum(spread, axis=1, keepdims=True), (32, 128))
    biases = remote(bias_own, bias_in, pair_send.at[2], pair_recv.at[2], partner)
    start(biases)

    gathered[:, slot_of(chan)] = keep[...]

    @pl.when(z_lo == 1)
    def _():
        for j in range(4):
            weights[0:9, 32:64, 128 * j : 128 * j + 128] = filt[:, :, lanes(j)]

    for part in range(2):
        pairs[part].wait_recv()
        for direction in range(2):
            start(ring(direction, 1, part, partner_chan, own_block(part, partner_chan)))
        send_halo(part, partner_chan, in_gathered(partner_chan))

    @pl.when(z_lo == 0)
    def _():
        for j in range(2):
            from_partner(j).start()

    def piece_wait(owner):
        slot = slot_of(owner)
        remote(packed.at[0], pieces.at[:, slot], piece_send.at[0], piece_recv.at[slot], partner).wait_recv()

    def owner_of(direction, hop):
        away = hop // 2 + 1
        base = (chan + 16 - 2 * away) % 16 if direction == 0 else (chan + 2 * away) % 16
        swap = hop % 2 == 1 if hop < 6 else direction == 1
        return base + 1 - 2 * z_lo if swap else base

    def multiply(half):
        lhs = weights[0:9, :, 256 * half : 256 * half + 256].reshape(576, 256)

        def body(q, carry):
            for n in range(2):
                columns = slice(256 * n, 256 * n + 256)
                rhs = gathered[q, 8 * half : 8 * half + 8, :, columns].reshape(256, 256)
                result = jnp.dot(lhs, rhs, preferred_element_type=F32).reshape(9, 64, 256)
                if half:
                    result = products[q, :, :, columns] + result
                products[q, :, :, columns] = result
            return carry

        lax.fori_loop(0, 4, body, 0)

    def multiply_halo(side, half):
        turned = (core + z_lo + side) % 2
        lhs = weights[pl.ds(6 * turned, 3), :, 256 * half : 256 * half + 256].reshape(192, 256)
        rhs = halo[side, 8 * half : 8 * half + 8].reshape(256, 512)
        result = jnp.dot(lhs, rhs, preferred_element_type=F32).reshape(3, 64, 512)
        if half:
            result = halo_products[side] + result
        halo_products[side] = result

    def halo_wait(side, half):
        for slot in range(8 * half, 8 * half + 8):
            remote(keep.at[0], halo.at[side, slot], halo_send.at[side, slot],
                   halo_recv.at[side, slot], twin).wait_recv()

    for hop in range(7):
        for part in range(2):
            for direction in range(2):
                owner = owner_of(direction, hop)
                ring(direction, hop, part, owner, keep.at[rows(part)]).wait_recv()
                onward = hop + 2 if hop < 4 or (hop == 4 and direction == 0) else None
                if hop == 5 and direction == 1:
                    onward = 6
                if onward is not None:
                    start(ring(direction, onward, part, owner, own_block(part, owner)))
                send_halo(part, owner, in_gathered(owner))
        if hop == 1:
            @pl.when(z_lo == 0)
            def _():
                for m in range(2):
                    owner = 2 * (x + 4 * m) + core
                    piece_wait(owner)
                    slot = slot_of(owner)
                    for k in range(1, 8):
                        remote(pieces.at[:, slot], pieces.at[:, slot], share_send.at[m, k],
                               piece_recv.at[slot], same_place(k)).start()

            @pl.when(z_lo == 1)
            def _():
                for j in range(2):
                    filters_wait(j, core)
                    hand_on(j).start()
        if hop == 3:
            @pl.when(z_lo == 0)
            def _():
                for k in range(1, 8):
                    band_of = same_place(k)["band"]
                    for m in range(2):
                        piece_wait(2 * ((band_of // 2) % 4 + 4 * m) + band_of % 2)
                for j in range(5):
                    weights[2 * j : 2 * j + 2] = pieces[j].reshape(512, 128).T.reshape(2, 64, 512)

            @pl.when(z_lo == 1)
            def _():
                for j in range(2):
                    filters_wait(j, 1 - core)
        if hop == 4:
            multiply(0)
        if hop == 5:
            halo_wait(1, 0)
            multiply_halo(1, 0)

            @pl.when(outer_ok)
            def _():
                halo_wait(0, 0)
                multiply_halo(0, 0)

            biases.wait_recv()

    multiply(1)

    column = lax.broadcasted_iota(jnp.int32, (64, 512), 1)
    offset = jnp.concatenate([bias_own[:, 0:1], bias_in[:, 0:1]], axis=0)
    offset = jnp.where(z_lo == 0, offset, jnp.zeros_like(offset))

    def tap(a, b):
        return 3 * a + b + z_lo * (8 - 2 * (3 * a + b))

    def finish(r, terms, side=None):
        sums = [sum(products[q, tap(a, b)] for q, a in terms) for b in range(3)]
        if side is not None:
            sums = [s + halo_products[side, b + z_lo * (2 - 2 * b)] for b, s in enumerate(sums)]
        left, mid, right = sums
        left = jnp.where(column == 0, 0.0, pltpu.roll(left, 1, 1))
        right = jnp.where(column == 511, 0.0, pltpu.roll(right, 511, 1))
        total = (left + mid + right + offset).astype(BF16)
        low, high = total[0:32], total[32:64]
        mine[r] = jnp.where(z_lo == 0, low, high)
        staged[r] = jnp.where(z_lo == 0, high, low)
        copy = remote(staged.at[r], other.at[r], out_send.at[r], out_recv.at[r], partner)
        copy.start()
        return copy

    outgoing = [finish(r, [(r + a - 1, a) for a in range(3)]) for r in (1, 2)]
    halo_wait(1, 1)
    multiply_halo(1, 1)
    outgoing.append(finish(3 - 3 * core, [(3 - 3 * core, 1), (2 - core, 2 * core)], 1))

    @pl.when(outer_ok)
    def _():
        halo_wait(0, 1)
        multiply_halo(0, 1)

    @pl.when(jnp.logical_not(outer_ok))
    def _():
        halo_products[0] = jnp.zeros((3, 64, 512), F32)

    outgoing.append(finish(3 * core, [(3 * core, 1), (1 + core, 2 - 2 * core)], 0))

    for copy in started:
        copy.wait_send()
    for slot in range(16):
        remote(keep.at[0], halo.at[1, slot], halo_send.at[1, slot], halo_recv.at[1, slot], twin).wait_send()

    @pl.when(outer_ok)
    def _():
        for slot in range(16):
            remote(keep.at[0], halo.at[0, slot], halo_send.at[0, slot], halo_recv.at[0, slot], twin).wait_send()

    @pl.when(sends_filters)
    def _():
        for d in range(1, 8):
            remote(packed.at[0], pieces.at[:, 0], piece_send.at[d], piece_recv.at[0], partner).wait_send()

        @pl.when(z_lo == 1)
        def _():
            remote(packed.at[0], pieces.at[:, 0], piece_send.at[0], piece_recv.at[0], partner).wait_send()

    @pl.when(z_lo == 0)
    def _():
        for j in range(2):
            from_partner(j).wait_send()
        for m in range(2):
            for k in range(1, 8):
                remote(pieces.at[:, 0], pieces.at[:, 0], share_send.at[m, k], piece_recv.at[0], partner).wait_send()

    @pl.when(z_lo == 1)
    def _():
        for j in range(2):
            hand_on(j).wait_send()

    for copy in outgoing:
        copy.wait()


def per_device(image, filters, bias, upstream):
    forward = lax.axis_index("chan") % 2 == 0
    rows_first = [jnp.transpose(value, (1, 0, 2)) for value in (image, upstream)]
    keep = jnp.where(forward, *rows_first)
    give = jnp.where(forward, *rows_first[::-1])
    filt = jnp.transpose(filters, (0, 2, 1))
    block = jax.ShapeDtypeStruct((4, 32, 512), BF16)
    vmem = pl.BlockSpec(memory_space=pltpu.VMEM)
    dma = pltpu.SemaphoreType.DMA
    mine, other = pl.pallas_call(
        kernel,
        out_shape=(block, block),
        in_specs=[vmem] * 4,
        out_specs=(vmem, vmem),
        scratch_shapes=[
            pltpu.VMEM((4, 16, 32, 512), BF16),
            pltpu.VMEM((2, 16, 32, 512), BF16),
            pltpu.VMEM((10, 64, 512), BF16),
            pltpu.VMEM((8, 5, 32, 128), BF16),
            pltpu.VMEM((5, 16, 32, 128), BF16),
            pltpu.VMEM((4, 9, 64, 512), F32),
            pltpu.VMEM((2, 3, 64, 512), F32),
            pltpu.VMEM((32, 128), F32),
            pltpu.VMEM((32, 128), F32),
            pltpu.VMEM((4, 32, 512), BF16),
            dma((2, 7, 2)), dma((2, 7, 2)), dma((3,)), dma((3,)), dma((2, 16)), dma((2, 16)),
            dma((2,)), dma((4,)), dma((2,)), dma((8,)), dma((16,)), dma((2, 8)),
            dma((4,)), dma((4,)),
        ],
        compiler_params=pltpu.CompilerParams(
            collective_id=0, has_side_effects=True, vmem_limit_bytes=40 << 20),
        name="conv_both",
    )(keep, give, filt, bias.reshape(1, 32))
    mine, other = (jnp.transpose(value, (1, 0, 2)) for value in (mine, other))
    return jnp.where(forward, mine, other), jnp.where(forward, other, mine)


def solution(mesh):
    return jax.shard_map(
        per_device,
        mesh=mesh,
        in_specs=(
            P("chan", "band", None),
            P(None, None, "chan"),
            P("chan"),
            P("chan", "band", None),
        ),
        out_specs=(P("chan", "band", None), P("chan", "band", None)),
        check_vma=False,
    )
```

```python
import jax
import jax.numpy as jnp
from jax import lax
from jax.experimental import pallas as pl
from jax.experimental.pallas import tpu as pltpu
from jax.sharding import PartitionSpec as P

MESH = pl.DeviceIdType.MESH
BF16, F32 = jnp.bfloat16, jnp.float32


POSITION = (0, 2, 3, 1)


def kernel(image, upstream, filters, bias_row, features, image_grad, natural, give, filt, bias,
           gathered, halo, weights, packed, pieces, products, halo_products, bias_own, bias_in,
           staged, load_sem, ring_send, ring_recv, pair_send, pair_recv, halo_send, halo_recv,
           filter_send, filter_recv, relay_send, piece_send, piece_recv, share_send,
           out_send, out_recv):
    band, chan = lax.axis_index("band"), lax.axis_index("chan")
    core, x, z_hi = band % 2, (band // 2) % 4, band // 8
    y, z_lo = chan // 2, chan % 2
    partner_chan = chan + 1 - 2 * z_lo
    partner = {"band": band, "chan": partner_chan}
    ring_next = ({"band": band, "chan": (chan + 2) % 16}, {"band": band, "chan": (chan + 14) % 16})
    twin = {"band": band + 1 - 2 * core, "chan": chan}
    outer_ok = ((core == 0) & (band > 0)) | ((core == 1) & (band < 31))
    outer = {"band": (band + 31 + 2 * core) % 32, "chan": chan}
    sends_filters = (core == z_lo) & (x == y % 4)

    def slot_at(owner, place):
        return (owner + 16 - 4 * (((place + 7) // 2) % 4)) % 16

    def slot_of(owner):
        return slot_at(owner, y)

    def remote(src, dst, send, recv, where):
        return pltpu.make_async_remote_copy(
            src_ref=src, dst_ref=dst, send_sem=send, recv_sem=recv,
            device_id=where, device_id_type=MESH)

    loads = [pltpu.make_async_copy(filters, filt, load_sem.at[2]),
             pltpu.make_async_copy(bias_row, bias, load_sem.at[3])]
    keeping = [pltpu.make_async_copy(image, natural.at[z_lo], load_sem.at[0]),
               pltpu.make_async_copy(upstream, natural.at[1 - z_lo], load_sem.at[1])]
    for copy in keeping + loads:
        copy.start()

    barrier = pltpu.get_barrier_semaphore()

    def greet(where):
        pl.semaphore_signal(barrier, inc=1, device_id=where, device_id_type=MESH)

    def other_x(k):
        return {"band": z_hi * 8 + ((x + k) % 4) * 2 + core, "chan": chan}

    inner = (x == 1) | (x == 2)
    gives_filters, takes_filters = (z_lo == 0) & inner, (z_lo == 1) & inner

    def at_x(place, unit):
        return {"band": z_hi * 8 + place * 2 + unit, "chan": chan}

    for where in (partner, *ring_next, twin):
        greet(where)

    @pl.when(outer_ok)
    def _():
        greet(outer)

    @pl.when(z_lo == 0)
    def _():
        for m in range(2):
            source = 2 * (x + 4 * m) + core

            @pl.when(source != chan)
            def _():
                greet({"band": band, "chan": source})
        for k in range(1, 4):
            greet(other_x(k))

    @pl.when((z_lo == 1) & jnp.logical_not(inner))
    def _():
        for unit in range(2):
            greet(at_x(1 + x // 2, unit))

    own_slot = slot_of(chan)
    for copy in keeping:
        copy.wait()
    for row in range(4):
        gathered[POSITION[row], own_slot] = natural[0, :, row, :]
        give[POSITION[row]] = natural[1, :, row, :]

    targets = 4 + jnp.where(outer_ok, 1, 0) + jnp.where(z_lo == 0, 3, 0)
    targets = targets + jnp.where(sends_filters, 7 + z_lo, 0) + jnp.where(takes_filters, 2, 0)
    pl.semaphore_wait(barrier, targets)

    def rows(part):
        return slice(2 * part, 2 * part + 2)

    def ring(direction, hop, part, owner, src):
        place = (y + 1) % 8 if direction == 0 else (y + 7) % 8
        return remote(src, gathered.at[rows(part), slot_at(owner, place)],
                      ring_send.at[direction, hop, part], ring_recv.at[direction, hop, part],
                      ring_next[direction])

    def own_block(part, owner):
        return gathered.at[rows(part), slot_of(owner)]

    def halo_copy(side, owner, src):
        slot = slot_of(owner)
        return remote(src, halo.at[side, slot], halo_send.at[side, slot],
                      halo_recv.at[side, slot], twin if side else outer)

    def send_halo(owner):
        slot = slot_of(owner)

        @pl.when(outer_ok)
        def _():
            halo_copy(0, owner, gathered.at[core, slot]).start()

        halo_copy(1, owner, gathered.at[1 - core, slot]).start()

    started = []

    def start(copy):
        copy.start()
        started.append(copy)

    pairs = [remote(give.at[rows(part)], gathered.at[rows(part), own_slot],
                    pair_send.at[part], pair_recv.at[part], partner) for part in range(2)]
    for part in range(2):
        start(pairs[part])
        for direction in range(2):
            start(ring(direction, 0, part, chan, own_block(part, chan)))
    send_halo(chan)
    for copy in loads:
        copy.wait()

    @pl.when(sends_filters)
    def _():
        lane = lax.broadcasted_iota(jnp.int32, (32, 128), 1)
        for q in range(4):
            for j in range(5):
                a = filt[2 * j, :, 128 * q : 128 * q + 128].astype(F32)
                b = filt[2 * j + 1, :, 128 * q : 128 * q + 128].astype(F32) if j < 4 else a
                packed[2 * q, j] = jnp.where(lane < 64, a, pltpu.roll(b, 64, 1)).astype(BF16)
                packed[2 * q + 1, j] = jnp.where(lane < 64, pltpu.roll(a, 64, 1), b).astype(BF16)
        for d in range(1, 8):
            place = (y + d) % 8
            slot = slot_at(chan, place)
            remote(packed.at[place], pieces.at[:, slot], piece_send.at[d],
                   piece_recv.at[slot], {"band": band, "chan": 2 * place}).start()
        slot = slot_of(chan)

        @pl.when(z_lo == 0)
        def _():
            pltpu.make_async_copy(packed.at[y], pieces.at[:, slot], piece_recv.at[slot]).start()

        @pl.when(z_lo == 1)
        def _():
            remote(packed.at[y], pieces.at[:, slot], piece_send.at[0],
                   piece_recv.at[slot], partner).start()

    turn = ((y + 7) // 2) % 4

    def lanes(j):
        return pl.ds(pl.multiple_of(128 * ((j + turn) % 4), 128), 128)

    def from_partner(j):
        column = pl.ds(pl.multiple_of(128 * (2 * core + j), 128), 128)
        return remote(filt.at[:, :, lanes(2 * core + j)], weights.at[0:9, 0:32, column],
                      filter_send.at[j], filter_recv.at[2 * core + j], partner)

    def hand_on(j, k):
        column = pl.ds(pl.multiple_of(128 * (2 * core + j), 128), 128)
        place = jnp.where(x == 1, 0, 3)
        return remote(weights.at[0:9, 0:32, column], weights.at[0:9, 0:32, column],
                      relay_send.at[j, k], filter_recv.at[2 * core + j],
                      (twin, at_x(place, 0), at_x(place, 1))[k])

    def filters_wait(j, unit):
        remote(filt.at[:, :, 0:128], weights.at[0:9, 0:32, 0:128],
               relay_send.at[j, 0], filter_recv.at[2 * unit + j], twin).wait_recv()

    diagonal = (lax.broadcasted_iota(jnp.int32, (32, 32), 0)
                == lax.broadcasted_iota(jnp.int32, (32, 32), 1))
    spread = jnp.where(diagonal, jnp.broadcast_to(bias[...].astype(F32), (32, 32)), 0.0)
    bias_own[...] = jnp.broadcast_to(jnp.sum(spread, axis=1, keepdims=True), (32, 128))
    biases = remote(bias_own, bias_in, pair_send.at[2], pair_recv.at[2], partner)
    start(biases)

    @pl.when(z_lo == 1)
    def _():
        for j in range(4):
            weights[0:9, 32:64, 128 * j : 128 * j + 128] = filt[:, :, lanes(j)]

    @pl.when(gives_filters)
    def _():
        for j in range(2):
            from_partner(j).start()

    def pair_arrived(part):
        pairs[part].wait_recv()
        for direction in range(2):
            start(ring(direction, 1, part, partner_chan, own_block(part, partner_chan)))
        if part == 0:
            send_halo(partner_chan)

    def piece_wait(owner):
        slot = slot_of(owner)
        remote(packed.at[0], pieces.at[:, slot], piece_send.at[0], piece_recv.at[slot], partner).wait_recv()

    def owner_of(direction, hop):
        away = hop // 2 + 1
        base = (chan + 16 - 2 * away) % 16 if direction == 0 else (chan + 2 * away) % 16
        swap = hop % 2 == 1 if hop < 6 else direction == 1
        return base + 1 - 2 * z_lo if swap else base

    def multiply(first, slots):
        lanes_of = slice(32 * slots[0], 32 * slots[1])
        depth = 32 * (slots[1] - slots[0])
        lhs = weights[0:9, :, lanes_of].reshape(576, depth)

        def body(q, carry):
            for n in range(2):
                columns = slice(256 * n, 256 * n + 256)
                rhs = gathered[q, slots[0] : slots[1], :, columns].reshape(depth, 256)
                result = jnp.dot(lhs, rhs, preferred_element_type=F32).reshape(9, 64, 256)
                if slots[0]:
                    result = products[q, :, :, columns] + result
                products[q, :, :, columns] = result
            return carry

        lax.fori_loop(first, first + 2, body, 0)

    def multiply_halo(side):
        for slot in range(16):
            remote(give.at[0], halo.at[side, slot], halo_send.at[side, slot],
                   halo_recv.at[side, slot], twin).wait_recv()
        turned = (core + z_lo + side) % 2
        lhs = weights[pl.ds(6 * turned, 3)].reshape(192, 512)
        rhs = halo[side].reshape(512, 512)
        halo_products[side] = jnp.dot(lhs, rhs, preferred_element_type=F32).reshape(3, 64, 512)

    def block_arrived(hop, part):
        for direction in range(2):
            owner = owner_of(direction, hop)
            ring(direction, hop, part, owner, give.at[rows(part)]).wait_recv()
            onward = hop + 2 if hop < 4 or (hop == 4 and direction == 0) else None
            if hop == 5 and direction == 1:
                onward = 6
            if onward is not None:
                start(ring(direction, onward, part, owner, own_block(part, owner)))
            if part == 0:
                send_halo(owner)

    def share_pieces():
        @pl.when(z_lo == 0)
        def _():
            for m in range(2):
                owner = 2 * (x + 4 * m) + core
                piece_wait(owner)
                slot = slot_of(owner)
                for k in range(4):
                    remote(pieces.at[:, slot], pieces.at[:, slot], share_send.at[m, k],
                           piece_recv.at[slot], other_x(k) if k else twin).start()

        @pl.when(takes_filters)
        def _():
            for j in range(2):
                filters_wait(j, core)
                for k in range(3):
                    hand_on(j, k).start()

    def hand_pieces():
        @pl.when(z_lo == 0)
        def _():
            for k in range(1, 4):
                for m in range(2):
                    owner = 2 * ((x + k) % 4 + 4 * m) + core
                    piece_wait(owner)
                    slot = slot_of(owner)
                    remote(pieces.at[:, slot], pieces.at[:, slot], share_send.at[m, 3 + k],
                           piece_recv.at[slot], twin).start()

    def take_filters():
        @pl.when(z_lo == 0)
        def _():
            for k in range(4):
                for m in range(2):
                    piece_wait(2 * (k + 4 * m) + 1 - core)
            for j in range(5):
                weights[2 * j : 2 * j + 2] = pieces[j].reshape(512, 128).T.reshape(2, 64, 512)

        @pl.when(z_lo == 1)
        def _():
            for j in range(2):
                filters_wait(j, 1 - core)

            @pl.when(jnp.logical_not(inner))
            def _():
                for j in range(2):
                    filters_wait(j, core)

    pair_arrived(0)
    block_arrived(0, 0)
    pair_arrived(1)
    block_arrived(0, 1)
    block_arrived(1, 0)
    block_arrived(1, 1)
    share_pieces()
    block_arrived(2, 0)
    block_arrived(2, 1)
    block_arrived(3, 0)
    block_arrived(3, 1)
    hand_pieces()
    block_arrived(4, 0)
    block_arrived(4, 1)
    block_arrived(5, 0)
    block_arrived(5, 1)
    take_filters()
    multiply(2, (0, 8))
    block_arrived(6, 0)
    multiply(0, (0, 16))
    multiply_halo(1)

    @pl.when(outer_ok)
    def _():
        multiply_halo(0)

    @pl.when(jnp.logical_not(outer_ok))
    def _():
        halo_products[0] = jnp.zeros((3, 64, 512), F32)

    biases.wait_recv()
    block_arrived(6, 1)
    multiply(2, (8, 16))

    column = lax.broadcasted_iota(jnp.int32, (64, 512), 1)
    offset = jnp.concatenate([bias_own[:, 0:1], bias_in[:, 0:1]], axis=0)
    offset = jnp.where(z_lo == 0, offset, jnp.zeros_like(offset))

    def tap(a, b):
        return 3 * a + b + z_lo * (8 - 2 * (3 * a + b))

    def finish(r, terms, side=None):
        sums = [sum(products[q, tap(a, b)] for q, a in terms) for b in range(3)]
        if side is not None:
            sums = [s + halo_products[side, b + z_lo * (2 - 2 * b)] for b, s in enumerate(sums)]
        left, mid, right = sums
        left = jnp.where(column == 0, 0.0, pltpu.roll(left, 1, 1))
        right = jnp.where(column == 511, 0.0, pltpu.roll(right, 511, 1))
        total = (left + mid + right + offset).astype(BF16)
        low, high = total[0:32], total[32:64]
        for side, own in ((0, features), (1, image_grad)):
            @pl.when(z_lo == side)
            def _():
                own[r] = high if side else low
                staged[r] = low if side else high
                remote(staged.at[r], own.at[r], out_send.at[r], out_recv.at[r], partner).start()
        return remote(staged.at[r], features.at[r], out_send.at[r], out_recv.at[r], partner)

    outgoing = [finish(r, [(POSITION[r + a - 1], a) for a in range(3)]) for r in (1, 2)]
    outgoing.append(finish(3 - 3 * core, [(1 - core, 1), (3 - core, 2 * core)], 1))
    outgoing.append(finish(3 * core, [(core, 1), (2 + core, 2 - 2 * core)], 0))

    for copy in started:
        copy.wait_send()
    for slot in range(16):
        remote(give.at[0], halo.at[1, slot], halo_send.at[1, slot], halo_recv.at[1, slot], twin).wait_send()

    @pl.when(outer_ok)
    def _():
        for slot in range(16):
            remote(give.at[0], halo.at[0, slot], halo_send.at[0, slot], halo_recv.at[0, slot], twin).wait_send()

    @pl.when(sends_filters)
    def _():
        for d in range(1, 8):
            remote(packed.at[0], pieces.at[:, 0], piece_send.at[d], piece_recv.at[0], partner).wait_send()

        @pl.when(z_lo == 1)
        def _():
            remote(packed.at[0], pieces.at[:, 0], piece_send.at[0], piece_recv.at[0], partner).wait_send()

    @pl.when(gives_filters)
    def _():
        for j in range(2):
            from_partner(j).wait_send()

    @pl.when(z_lo == 0)
    def _():
        for m in range(2):
            for k in range(7):
                remote(pieces.at[:, 0], pieces.at[:, 0], share_send.at[m, k], piece_recv.at[0], partner).wait_send()

    @pl.when(takes_filters)
    def _():
        for j in range(2):
            for k in range(3):
                hand_on(j, k).wait_send()

    for copy in outgoing:
        copy.wait()


def per_device(image, filters, bias, upstream):
    filt = jnp.transpose(filters, (0, 2, 1))
    block = jax.ShapeDtypeStruct((4, 32, 512), BF16)
    dma = pltpu.SemaphoreType.DMA
    features, image_grad = pl.pallas_call(
        kernel,
        out_shape=(block, block),
        in_specs=[pl.BlockSpec(memory_space=pltpu.HBM)] * 4,
        out_specs=(pl.BlockSpec(memory_space=pltpu.VMEM),) * 2,
        scratch_shapes=[
            pltpu.VMEM((2, 32, 4, 512), BF16),
            pltpu.VMEM((4, 32, 512), BF16),
            pltpu.VMEM((9, 32, 512), BF16),
            pltpu.VMEM((1, 32), BF16),
            pltpu.VMEM((4, 16, 32, 512), BF16),
            pltpu.VMEM((2, 16, 32, 512), BF16),
            pltpu.VMEM((10, 64, 512), BF16),
            pltpu.VMEM((8, 5, 32, 128), BF16),
            pltpu.VMEM((5, 16, 32, 128), BF16),
            pltpu.VMEM((4, 9, 64, 512), F32),
            pltpu.VMEM((2, 3, 64, 512), F32),
            pltpu.VMEM((32, 128), F32),
            pltpu.VMEM((32, 128), F32),
            pltpu.VMEM((4, 32, 512), BF16),
            dma((4,)), dma((2, 7, 2)), dma((2, 7, 2)), dma((3,)), dma((3,)), dma((2, 16)), dma((2, 16)),
            dma((2,)), dma((4,)), dma((2, 3)), dma((8,)), dma((16,)), dma((2, 7)),
            dma((4,)), dma((4,)),
        ],
        compiler_params=pltpu.CompilerParams(
            collective_id=0, has_side_effects=True, vmem_limit_bytes=40 << 20),
        name="conv_both",
    )(*(pltpu.with_memory_space_constraint(value, pltpu.HBM)
        for value in (image, upstream, filt, bias.reshape(1, 32))))
    return tuple(jnp.transpose(value, (1, 0, 2)) for value in (features, image_grad))


def solution(mesh):
    return jax.shard_map(
        per_device,
        mesh=mesh,
        in_specs=(
            P("chan", "band", None),
            P(None, None, "chan"),
            P("chan"),
            P("chan", "band", None),
        ),
        out_specs=(P("chan", "band", None), P("chan", "band", None)),
        check_vma=False,
    )
```

```python
import jax
import jax.numpy as jnp
from jax import lax
from jax.experimental import pallas as pl
from jax.experimental.pallas import tpu as pltpu
from jax.sharding import PartitionSpec as P

MESH = pl.DeviceIdType.MESH
BF16, F32 = jnp.bfloat16, jnp.float32


POSITION = (0, 2, 3, 1)


def kernel(image, upstream, filters, bias_row, features, image_grad, natural, give, filt, bias,
           gathered, halo, weights, packed, pieces, products, halo_products, bias_own, bias_in,
           staged, load_sem, ring_send, ring_recv, pair_send, pair_recv, halo_send, halo_recv,
           filter_send, filter_recv, relay_send, piece_send, piece_recv, share_send,
           out_send, out_recv):
    band, chan = lax.axis_index("band"), lax.axis_index("chan")
    core, x, z_hi = band % 2, (band // 2) % 4, band // 8
    y, z_lo = chan // 2, chan % 2
    partner_chan = chan + 1 - 2 * z_lo
    partner = {"band": band, "chan": partner_chan}
    ring_next = ({"band": band, "chan": (chan + 2) % 16}, {"band": band, "chan": (chan + 14) % 16})
    twin = {"band": band + 1 - 2 * core, "chan": chan}
    outer_ok = ((core == 0) & (band > 0)) | ((core == 1) & (band < 31))
    outer = {"band": (band + 31 + 2 * core) % 32, "chan": chan}
    sends_filters = (core == z_lo) & (x == y % 4)

    def slot_at(owner, place):
        return (owner + 16 - 4 * (((place + 7) // 2) % 4)) % 16

    def slot_of(owner):
        return slot_at(owner, y)

    def remote(src, dst, send, recv, where):
        return pltpu.make_async_remote_copy(
            src_ref=src, dst_ref=dst, send_sem=send, recv_sem=recv,
            device_id=where, device_id_type=MESH)

    loads = [pltpu.make_async_copy(filters, filt, load_sem.at[2]),
             pltpu.make_async_copy(bias_row, bias, load_sem.at[3])]
    keeping = [pltpu.make_async_copy(image, natural.at[z_lo], load_sem.at[0]),
               pltpu.make_async_copy(upstream, natural.at[1 - z_lo], load_sem.at[1])]
    for copy in keeping + loads:
        copy.start()

    barrier = pltpu.get_barrier_semaphore()

    def greet(where):
        pl.semaphore_signal(barrier, inc=1, device_id=where, device_id_type=MESH)

    def other_x(k):
        return {"band": z_hi * 8 + ((x + k) % 4) * 2 + core, "chan": chan}

    inner = (x == 1) | (x == 2)
    gives_filters, takes_filters = (z_lo == 0) & inner, (z_lo == 1) & inner

    def at_x(place, unit):
        return {"band": z_hi * 8 + place * 2 + unit, "chan": chan}

    for where in (partner, *ring_next, twin):
        greet(where)

    @pl.when(outer_ok)
    def _():
        greet(outer)

    @pl.when(z_lo == 0)
    def _():
        for m in range(2):
            source = 2 * (x + 4 * m) + core

            @pl.when(source != chan)
            def _():
                greet({"band": band, "chan": source})
        for k in range(1, 4):
            greet(other_x(k))

    @pl.when((z_lo == 1) & jnp.logical_not(inner))
    def _():
        for unit in range(2):
            greet(at_x(1 + x // 2, unit))

    own_slot = slot_of(chan)
    for copy in keeping:
        copy.wait()
    for row in range(4):
        gathered[POSITION[row], own_slot] = natural[0, :, row, :]
        give[POSITION[row]] = natural[1, :, row, :]

    targets = 4 + jnp.where(outer_ok, 1, 0) + jnp.where(z_lo == 0, 3, 0)
    targets = targets + jnp.where(sends_filters, 7 + z_lo, 0) + jnp.where(takes_filters, 2, 0)
    pl.semaphore_wait(barrier, targets)

    def rows(part):
        return slice(2 * part, 2 * part + 2)

    def ring(direction, hop, part, owner, src):
        place = (y + 1) % 8 if direction == 0 else (y + 7) % 8
        return remote(src, gathered.at[rows(part), slot_at(owner, place)],
                      ring_send.at[direction, hop, part], ring_recv.at[direction, hop, part],
                      ring_next[direction])

    def own_block(part, owner):
        return gathered.at[rows(part), slot_of(owner)]

    def halo_copy(side, owner, src):
        slot = slot_of(owner)
        return remote(src, halo.at[side, slot], halo_send.at[side, slot],
                      halo_recv.at[side, slot], twin if side else outer)

    def send_halo(owner):
        slot = slot_of(owner)

        @pl.when(outer_ok)
        def _():
            halo_copy(0, owner, gathered.at[core, slot]).start()

        halo_copy(1, owner, gathered.at[1 - core, slot]).start()

    started = []

    def start(copy):
        copy.start()
        started.append(copy)

    pairs = [remote(give.at[rows(part)], gathered.at[rows(part), own_slot],
                    pair_send.at[part], pair_recv.at[part], partner) for part in range(2)]
    for part in range(2):
        start(pairs[part])
        for direction in range(2):
            start(ring(direction, 0, part, chan, own_block(part, chan)))
    send_halo(chan)
    turn = ((y + 7) // 2) % 4

    def lanes(j):
        return pl.ds(pl.multiple_of(128 * ((j + turn) % 4), 128), 128)

    def from_partner(j):
        column = pl.ds(pl.multiple_of(128 * (2 * core + j), 128), 128)
        return remote(filt.at[:, :, lanes(2 * core + j)], weights.at[0:9, 0:32, column],
                      filter_send.at[j], filter_recv.at[2 * core + j], partner)

    def hand_on(j, k):
        column = pl.ds(pl.multiple_of(128 * (2 * core + j), 128), 128)
        place = jnp.where(x == 1, 0, 3)
        return remote(weights.at[0:9, 0:32, column], weights.at[0:9, 0:32, column],
                      relay_send.at[j, k], filter_recv.at[2 * core + j],
                      (twin, at_x(place, 0), at_x(place, 1))[k])

    def filters_wait(j, unit):
        remote(filt.at[:, :, 0:128], weights.at[0:9, 0:32, 0:128],
               relay_send.at[j, 0], filter_recv.at[2 * unit + j], twin).wait_recv()

    biases = remote(bias_own, bias_in, pair_send.at[2], pair_recv.at[2], partner)

    def prepare():
        for copy in loads:
            copy.wait()

        @pl.when(sends_filters)
        def _():
            lane = lax.broadcasted_iota(jnp.int32, (32, 128), 1)
            for q in range(4):
                for j in range(5):
                    a = filt[2 * j, :, 128 * q : 128 * q + 128].astype(F32)
                    b = filt[2 * j + 1, :, 128 * q : 128 * q + 128].astype(F32) if j < 4 else a
                    packed[2 * q, j] = jnp.where(lane < 64, a, pltpu.roll(b, 64, 1)).astype(BF16)
                    packed[2 * q + 1, j] = jnp.where(lane < 64, pltpu.roll(a, 64, 1), b).astype(BF16)
            for d in range(1, 8):
                place = (y + d) % 8
                slot = slot_at(chan, place)
                remote(packed.at[place], pieces.at[:, slot], piece_send.at[d],
                       piece_recv.at[slot], {"band": band, "chan": 2 * place}).start()
            slot = slot_of(chan)

            @pl.when(z_lo == 0)
            def _():
                pltpu.make_async_copy(packed.at[y], pieces.at[:, slot], piece_recv.at[slot]).start()

            @pl.when(z_lo == 1)
            def _():
                remote(packed.at[y], pieces.at[:, slot], piece_send.at[0],
                       piece_recv.at[slot], partner).start()

        diagonal = (lax.broadcasted_iota(jnp.int32, (32, 32), 0)
                    == lax.broadcasted_iota(jnp.int32, (32, 32), 1))
        spread = jnp.where(diagonal, jnp.broadcast_to(bias[...].astype(F32), (32, 32)), 0.0)
        bias_own[...] = jnp.broadcast_to(jnp.sum(spread, axis=1, keepdims=True), (32, 128))
        start(biases)

        @pl.when(z_lo == 1)
        def _():
            for j in range(4):
                weights[0:9, 32:64, 128 * j : 128 * j + 128] = filt[:, :, lanes(j)]

        @pl.when(gives_filters)
        def _():
            for j in range(2):
                from_partner(j).start()

    def pair_arrived(part):
        pairs[part].wait_recv()
        for direction in range(2):
            start(ring(direction, 1, part, partner_chan, own_block(part, partner_chan)))
        if part == 0:
            send_halo(partner_chan)

    def piece_wait(owner):
        slot = slot_of(owner)
        remote(packed.at[0], pieces.at[:, slot], piece_send.at[0], piece_recv.at[slot], partner).wait_recv()

    def owner_of(direction, hop):
        away = hop // 2 + 1
        base = (chan + 16 - 2 * away) % 16 if direction == 0 else (chan + 2 * away) % 16
        swap = hop % 2 == 1 if hop < 6 else direction == 1
        return base + 1 - 2 * z_lo if swap else base

    def multiply(first, slots):
        lanes_of = slice(32 * slots[0], 32 * slots[1])
        depth = 32 * (slots[1] - slots[0])
        lhs = weights[0:9, :, lanes_of].reshape(576, depth)

        def body(q, carry):
            for n in range(2):
                columns = slice(256 * n, 256 * n + 256)
                rhs = gathered[q, slots[0] : slots[1], :, columns].reshape(depth, 256)
                result = jnp.dot(lhs, rhs, preferred_element_type=F32).reshape(9, 64, 256)
                if slots[0]:
                    result = products[q, :, :, columns] + result
                products[q, :, :, columns] = result
            return carry

        lax.fori_loop(first, first + 2, body, 0)

    def multiply_halo(side):
        for slot in range(16):
            remote(give.at[0], halo.at[side, slot], halo_send.at[side, slot],
                   halo_recv.at[side, slot], twin).wait_recv()
        turned = (core + z_lo + side) % 2
        lhs = weights[pl.ds(6 * turned, 3)].reshape(192, 512)
        rhs = halo[side].reshape(512, 512)
        halo_products[side] = jnp.dot(lhs, rhs, preferred_element_type=F32).reshape(3, 64, 512)

    def block_arrived(hop, part):
        for direction in range(2):
            owner = owner_of(direction, hop)
            ring(direction, hop, part, owner, give.at[rows(part)]).wait_recv()
            onward = hop + 2 if hop < 4 or (hop == 4 and direction == 0) else None
            if hop == 5 and direction == 1:
                onward = 6
            if onward is not None:
                start(ring(direction, onward, part, owner, own_block(part, owner)))
            if part == 0:
                send_halo(owner)

    def share_pieces():
        @pl.when(z_lo == 0)
        def _():
            for m in range(2):
                owner = 2 * (x + 4 * m) + core
                piece_wait(owner)
                slot = slot_of(owner)
                for k in range(4):
                    remote(pieces.at[:, slot], pieces.at[:, slot], share_send.at[m, k],
                           piece_recv.at[slot], other_x(k) if k else twin).start()

        @pl.when(takes_filters)
        def _():
            for j in range(2):
                filters_wait(j, core)
                for k in range(3):
                    hand_on(j, k).start()

    def hand_pieces():
        @pl.when(z_lo == 0)
        def _():
            for k in range(1, 4):
                for m in range(2):
                    owner = 2 * ((x + k) % 4 + 4 * m) + core
                    piece_wait(owner)
                    slot = slot_of(owner)
                    remote(pieces.at[:, slot], pieces.at[:, slot], share_send.at[m, 3 + k],
                           piece_recv.at[slot], twin).start()

    def take_filters():
        @pl.when(z_lo == 0)
        def _():
            for k in range(4):
                for m in range(2):
                    piece_wait(2 * (k + 4 * m) + 1 - core)
            for j in range(5):
                weights[2 * j : 2 * j + 2] = pieces[j].reshape(512, 128).T.reshape(2, 64, 512)

        @pl.when(z_lo == 1)
        def _():
            for j in range(2):
                filters_wait(j, 1 - core)

            @pl.when(jnp.logical_not(inner))
            def _():
                for j in range(2):
                    filters_wait(j, core)

    prepare()
    pair_arrived(0)
    block_arrived(0, 0)
    pair_arrived(1)
    block_arrived(1, 0)
    block_arrived(0, 1)
    block_arrived(2, 0)
    block_arrived(1, 1)
    share_pieces()
    block_arrived(3, 0)
    block_arrived(2, 1)
    block_arrived(4, 0)
    block_arrived(3, 1)
    hand_pieces()
    block_arrived(5, 0)
    block_arrived(4, 1)
    block_arrived(6, 0)
    block_arrived(5, 1)
    take_filters()
    multiply(2, (0, 8))
    multiply(0, (0, 16))
    multiply_halo(1)
    biases.wait_recv()
    block_arrived(6, 1)
    multiply(2, (8, 16))

    column = lax.broadcasted_iota(jnp.int32, (64, 512), 1)
    offset = jnp.concatenate([bias_own[:, 0:1], bias_in[:, 0:1]], axis=0)
    offset = jnp.where(z_lo == 0, offset, jnp.zeros_like(offset))

    def tap(a, b):
        return 3 * a + b + z_lo * (8 - 2 * (3 * a + b))

    def finish(r, terms, side=None):
        sums = [sum(products[q, tap(a, b)] for q, a in terms) for b in range(3)]
        if side is not None:
            sums = [s + halo_products[side, b + z_lo * (2 - 2 * b)] for b, s in enumerate(sums)]
        left, mid, right = sums
        left = jnp.where(column == 0, 0.0, pltpu.roll(left, 1, 1))
        right = jnp.where(column == 511, 0.0, pltpu.roll(right, 511, 1))
        total = (left + mid + right + offset).astype(BF16)
        low, high = total[0:32], total[32:64]
        for side, own in ((0, features), (1, image_grad)):
            @pl.when(z_lo == side)
            def _():
                own[r] = high if side else low
                staged[r] = low if side else high
                remote(staged.at[r], own.at[r], out_send.at[r], out_recv.at[r], partner).start()
        return remote(staged.at[r], features.at[r], out_send.at[r], out_recv.at[r], partner)

    outgoing = [finish(r, [(POSITION[r + a - 1], a) for a in range(3)]) for r in (1, 2)]
    outgoing.append(finish(3 - 3 * core, [(1 - core, 1), (3 - core, 2 * core)], 1))

    @pl.when(outer_ok)
    def _():
        multiply_halo(0)

    @pl.when(jnp.logical_not(outer_ok))
    def _():
        halo_products[0] = jnp.zeros((3, 64, 512), F32)

    outgoing.append(finish(3 * core, [(core, 1), (2 + core, 2 - 2 * core)], 0))

    for copy in started:
        copy.wait_send()
    for slot in range(16):
        remote(give.at[0], halo.at[1, slot], halo_send.at[1, slot], halo_recv.at[1, slot], twin).wait_send()

    @pl.when(outer_ok)
    def _():
        for slot in range(16):
            remote(give.at[0], halo.at[0, slot], halo_send.at[0, slot], halo_recv.at[0, slot], twin).wait_send()

    @pl.when(sends_filters)
    def _():
        for d in range(1, 8):
            remote(packed.at[0], pieces.at[:, 0], piece_send.at[d], piece_recv.at[0], partner).wait_send()

        @pl.when(z_lo == 1)
        def _():
            remote(packed.at[0], pieces.at[:, 0], piece_send.at[0], piece_recv.at[0], partner).wait_send()

    @pl.when(gives_filters)
    def _():
        for j in range(2):
            from_partner(j).wait_send()

    @pl.when(z_lo == 0)
    def _():
        for m in range(2):
            for k in range(7):
                remote(pieces.at[:, 0], pieces.at[:, 0], share_send.at[m, k], piece_recv.at[0], partner).wait_send()

    @pl.when(takes_filters)
    def _():
        for j in range(2):
            for k in range(3):
                hand_on(j, k).wait_send()

    for copy in outgoing:
        copy.wait()


def per_device(image, filters, bias, upstream):
    filt = jnp.transpose(filters, (0, 2, 1))
    block = jax.ShapeDtypeStruct((4, 32, 512), BF16)
    dma = pltpu.SemaphoreType.DMA
    features, image_grad = pl.pallas_call(
        kernel,
        out_shape=(block, block),
        in_specs=[pl.BlockSpec(memory_space=pltpu.HBM)] * 4,
        out_specs=(pl.BlockSpec(memory_space=pltpu.VMEM),) * 2,
        scratch_shapes=[
            pltpu.VMEM((2, 32, 4, 512), BF16),
            pltpu.VMEM((4, 32, 512), BF16),
            pltpu.VMEM((9, 32, 512), BF16),
            pltpu.VMEM((1, 32), BF16),
            pltpu.VMEM((4, 16, 32, 512), BF16),
            pltpu.VMEM((2, 16, 32, 512), BF16),
            pltpu.VMEM((10, 64, 512), BF16),
            pltpu.VMEM((8, 5, 32, 128), BF16),
            pltpu.VMEM((5, 16, 32, 128), BF16),
            pltpu.VMEM((4, 9, 64, 512), F32),
            pltpu.VMEM((2, 3, 64, 512), F32),
            pltpu.VMEM((32, 128), F32),
            pltpu.VMEM((32, 128), F32),
            pltpu.VMEM((4, 32, 512), BF16),
            dma((4,)), dma((2, 7, 2)), dma((2, 7, 2)), dma((3,)), dma((3,)), dma((2, 16)), dma((2, 16)),
            dma((2,)), dma((4,)), dma((2, 3)), dma((8,)), dma((16,)), dma((2, 7)),
            dma((4,)), dma((4,)),
        ],
        compiler_params=pltpu.CompilerParams(
            collective_id=0, has_side_effects=True, vmem_limit_bytes=40 << 20),
        name="conv_both",
    )(*(pltpu.with_memory_space_constraint(value, pltpu.HBM)
        for value in (image, upstream, filt, bias.reshape(1, 32))))
    return tuple(jnp.transpose(value, (1, 0, 2)) for value in (features, image_grad))


def solution(mesh):
    return jax.shard_map(
        per_device,
        mesh=mesh,
        in_specs=(
            P("chan", "band", None),
            P(None, None, "chan"),
            P("chan"),
            P("chan", "band", None),
        ),
        out_specs=(P("chan", "band", None), P("chan", "band", None)),
        check_vma=False,
    )
```

```python
import jax
import jax.numpy as jnp
from jax import lax
from jax.experimental import pallas as pl
from jax.experimental.pallas import tpu as pltpu
from jax.sharding import PartitionSpec as P

MESH = pl.DeviceIdType.MESH
BF16, F32 = jnp.bfloat16, jnp.float32


POSITION = (0, 2, 3, 1)


def kernel(image, upstream, filters, bias_row, features, image_grad, natural, give, filt, bias,
           gathered, halo, weights, packed, pieces, products, halo_products, bias_own, bias_in,
           staged, load_sem, ring_send, ring_recv, pair_send, pair_recv, halo_send, halo_recv,
           filter_send, filter_recv, relay_send, piece_send, piece_recv, share_send,
           out_send, out_recv):
    band, chan = lax.axis_index("band"), lax.axis_index("chan")
    core, x, z_hi = band % 2, (band // 2) % 4, band // 8
    y, z_lo = chan // 2, chan % 2
    partner_chan = chan + 1 - 2 * z_lo
    partner = {"band": band, "chan": partner_chan}
    ring_next = ({"band": band, "chan": (chan + 2) % 16}, {"band": band, "chan": (chan + 14) % 16})
    twin = {"band": band + 1 - 2 * core, "chan": chan}
    outer_ok = ((core == 0) & (band > 0)) | ((core == 1) & (band < 31))
    outer = {"band": (band + 31 + 2 * core) % 32, "chan": chan}
    sends_filters = (core == z_lo) & (x == y % 4)

    def slot_at(owner, place):
        return (owner + 16 - 4 * (((place + 7) // 2) % 4)) % 16

    def slot_of(owner):
        return slot_at(owner, y)

    def remote(src, dst, send, recv, where):
        return pltpu.make_async_remote_copy(
            src_ref=src, dst_ref=dst, send_sem=send, recv_sem=recv,
            device_id=where, device_id_type=MESH)

    loads = [pltpu.make_async_copy(filters, filt, load_sem.at[2]),
             pltpu.make_async_copy(bias_row, bias, load_sem.at[3])]
    keeping = [pltpu.make_async_copy(image, natural.at[z_lo], load_sem.at[0]),
               pltpu.make_async_copy(upstream, natural.at[1 - z_lo], load_sem.at[1])]
    for copy in keeping + loads:
        copy.start()

    barrier = pltpu.get_barrier_semaphore()

    def greet(where):
        pl.semaphore_signal(barrier, inc=1, device_id=where, device_id_type=MESH)

    def other_x(k):
        return {"band": z_hi * 8 + ((x + k) % 4) * 2 + core, "chan": chan}

    inner = (x == 1) | (x == 2)
    gives_filters, takes_filters = (z_lo == 0) & inner, (z_lo == 1) & inner

    def at_x(place, unit):
        return {"band": z_hi * 8 + place * 2 + unit, "chan": chan}

    for where in (partner, *ring_next, twin):
        greet(where)

    @pl.when(outer_ok)
    def _():
        greet(outer)

    @pl.when(z_lo == 0)
    def _():
        for m in range(2):
            source = 2 * (x + 4 * m) + core

            @pl.when(source != chan)
            def _():
                greet({"band": band, "chan": source})
        for k in range(1, 4):
            greet(other_x(k))

    @pl.when((z_lo == 1) & jnp.logical_not(inner))
    def _():
        for unit in range(2):
            greet(at_x(1 + x // 2, unit))

    own_slot = slot_of(chan)
    for copy in keeping:
        copy.wait()
    for row in range(4):
        gathered[POSITION[row], own_slot] = natural[0, :, row, :]
        give[POSITION[row]] = natural[1, :, row, :]

    targets = 4 + jnp.where(outer_ok, 1, 0) + jnp.where(z_lo == 0, 3, 0)
    targets = targets + jnp.where(sends_filters, 7 + z_lo, 0) + jnp.where(takes_filters, 2, 0)
    pl.semaphore_wait(barrier, targets)

    def rows(part):
        return slice(2 * part, 2 * part + 2)

    def ring(direction, hop, part, owner, src):
        place = (y + 1) % 8 if direction == 0 else (y + 7) % 8
        return remote(src, gathered.at[rows(part), slot_at(owner, place)],
                      ring_send.at[direction, hop, part], ring_recv.at[direction, hop, part],
                      ring_next[direction])

    def own_block(part, owner):
        return gathered.at[rows(part), slot_of(owner)]

    def halo_copy(side, owner, src):
        slot = slot_of(owner)
        return remote(src, halo.at[side, slot], halo_send.at[side, slot],
                      halo_recv.at[side, slot], twin if side else outer)

    def send_halo(owner):
        slot = slot_of(owner)

        @pl.when(outer_ok)
        def _():
            halo_copy(0, owner, gathered.at[core, slot]).start()

        halo_copy(1, owner, gathered.at[1 - core, slot]).start()

    started = []

    def start(copy):
        copy.start()
        started.append(copy)

    pairs = [remote(give.at[rows(part)], gathered.at[rows(part), own_slot],
                    pair_send.at[part], pair_recv.at[part], partner) for part in range(2)]
    for part in range(2):
        start(pairs[part])
        for direction in range(2):
            start(ring(direction, 0, part, chan, own_block(part, chan)))
    send_halo(chan)
    turn = ((y + 7) // 2) % 4

    def lanes(j):
        return pl.ds(pl.multiple_of(128 * ((j + turn) % 4), 128), 128)

    def from_partner(j):
        column = pl.ds(pl.multiple_of(128 * (2 * core + j), 128), 128)
        return remote(filt.at[:, :, lanes(2 * core + j)], weights.at[0:9, 0:32, column],
                      filter_send.at[j], filter_recv.at[2 * core + j], partner)

    def hand_on(j, k):
        column = pl.ds(pl.multiple_of(128 * (2 * core + j), 128), 128)
        place = jnp.where(x == 1, 0, 3)
        return remote(weights.at[0:9, 0:32, column], weights.at[0:9, 0:32, column],
                      relay_send.at[j, k], filter_recv.at[2 * core + j],
                      (twin, at_x(place, 0), at_x(place, 1))[k])

    def filters_wait(j, unit):
        remote(filt.at[:, :, 0:128], weights.at[0:9, 0:32, 0:128],
               relay_send.at[j, 0], filter_recv.at[2 * unit + j], twin).wait_recv()

    biases = remote(bias_own, bias_in, pair_send.at[2], pair_recv.at[2], partner)

    def prepare():
        for copy in loads:
            copy.wait()

        @pl.when(sends_filters)
        def _():
            lane = lax.broadcasted_iota(jnp.int32, (32, 128), 1)
            for q in range(4):
                for j in range(5):
                    a = filt[2 * j, :, 128 * q : 128 * q + 128].astype(F32)
                    b = filt[2 * j + 1, :, 128 * q : 128 * q + 128].astype(F32) if j < 4 else a
                    packed[2 * q, j] = jnp.where(lane < 64, a, pltpu.roll(b, 64, 1)).astype(BF16)
                    packed[2 * q + 1, j] = jnp.where(lane < 64, pltpu.roll(a, 64, 1), b).astype(BF16)
            for d in range(1, 8):
                place = (y + d) % 8
                slot = slot_at(chan, place)
                remote(packed.at[place], pieces.at[:, slot], piece_send.at[d],
                       piece_recv.at[slot], {"band": band, "chan": 2 * place}).start()
            slot = slot_of(chan)

            @pl.when(z_lo == 0)
            def _():
                pltpu.make_async_copy(packed.at[y], pieces.at[:, slot], piece_recv.at[slot]).start()

            @pl.when(z_lo == 1)
            def _():
                remote(packed.at[y], pieces.at[:, slot], piece_send.at[0],
                       piece_recv.at[slot], partner).start()

        diagonal = (lax.broadcasted_iota(jnp.int32, (32, 32), 0)
                    == lax.broadcasted_iota(jnp.int32, (32, 32), 1))
        spread = jnp.where(diagonal, jnp.broadcast_to(bias[...].astype(F32), (32, 32)), 0.0)
        bias_own[...] = jnp.broadcast_to(jnp.sum(spread, axis=1, keepdims=True), (32, 128))
        start(biases)

        @pl.when(z_lo == 1)
        def _():
            for j in range(4):
                weights[0:9, 32:64, 128 * j : 128 * j + 128] = filt[:, :, lanes(j)]

        @pl.when(gives_filters)
        def _():
            for j in range(2):
                from_partner(j).start()

    def pair_arrived(part):
        pairs[part].wait_recv()
        for direction in range(2):
            start(ring(direction, 1, part, partner_chan, own_block(part, partner_chan)))
        if part == 0:
            send_halo(partner_chan)

    def piece_wait(owner):
        slot = slot_of(owner)
        remote(packed.at[0], pieces.at[:, slot], piece_send.at[0], piece_recv.at[slot], partner).wait_recv()

    def owner_of(direction, hop):
        away = hop // 2 + 1
        base = (chan + 16 - 2 * away) % 16 if direction == 0 else (chan + 2 * away) % 16
        swap = hop % 2 == 1 if hop < 6 else direction == 1
        return base + 1 - 2 * z_lo if swap else base

    def multiply(first, slots):
        lanes_of = slice(32 * slots[0], 32 * slots[1])
        depth = 32 * (slots[1] - slots[0])
        lhs = weights[0:9, :, lanes_of].reshape(576, depth)

        def body(q, carry):
            for n in range(2):
                columns = slice(256 * n, 256 * n + 256)
                rhs = gathered[q, slots[0] : slots[1], :, columns].reshape(depth, 256)
                result = jnp.dot(lhs, rhs, preferred_element_type=F32).reshape(9, 64, 256)
                if slots[0]:
                    result = products[q, :, :, columns] + result
                products[q, :, :, columns] = result
            return carry

        lax.fori_loop(first, first + 2, body, 0)

    def multiply_halo(side):
        for slot in range(16):
            remote(give.at[0], halo.at[side, slot], halo_send.at[side, slot],
                   halo_recv.at[side, slot], twin).wait_recv()
        turned = (core + z_lo + side) % 2
        lhs = weights[pl.ds(6 * turned, 3)].reshape(192, 512)
        rhs = halo[side].reshape(512, 512)
        halo_products[side] = jnp.dot(lhs, rhs, preferred_element_type=F32).reshape(3, 64, 512)

    def block_arrived(hop, part):
        for direction in range(2):
            owner = owner_of(direction, hop)
            ring(direction, hop, part, owner, give.at[rows(part)]).wait_recv()
            onward = hop + 2 if hop < 4 or (hop == 4 and direction == 0) else None
            if hop == 5 and direction == 1:
                onward = 6
            if onward is not None:
                start(ring(direction, onward, part, owner, own_block(part, owner)))
            if part == 0:
                send_halo(owner)

    def share_pieces():
        @pl.when(z_lo == 0)
        def _():
            for m in range(2):
                owner = 2 * (x + 4 * m) + core
                piece_wait(owner)
                slot = slot_of(owner)
                for k in range(4):
                    remote(pieces.at[:, slot], pieces.at[:, slot], share_send.at[m, k],
                           piece_recv.at[slot], other_x(k) if k else twin).start()

        @pl.when(takes_filters)
        def _():
            for j in range(2):
                filters_wait(j, core)
                for k in range(3):
                    hand_on(j, k).start()

    def hand_pieces():
        @pl.when(z_lo == 0)
        def _():
            for k in range(1, 4):
                for m in range(2):
                    owner = 2 * ((x + k) % 4 + 4 * m) + core
                    piece_wait(owner)
                    slot = slot_of(owner)
                    remote(pieces.at[:, slot], pieces.at[:, slot], share_send.at[m, 3 + k],
                           piece_recv.at[slot], twin).start()

    def take_filters():
        @pl.when(z_lo == 0)
        def _():
            for k in range(4):
                for m in range(2):
                    piece_wait(2 * (k + 4 * m) + 1 - core)
            for j in range(5):
                weights[2 * j : 2 * j + 2] = pieces[j].reshape(512, 128).T.reshape(2, 64, 512)

        @pl.when(z_lo == 1)
        def _():
            for j in range(2):
                filters_wait(j, 1 - core)

            @pl.when(jnp.logical_not(inner))
            def _():
                for j in range(2):
                    filters_wait(j, core)

    prepare()
    pair_arrived(0)
    block_arrived(0, 0)
    pair_arrived(1)
    block_arrived(1, 0)
    block_arrived(0, 1)
    block_arrived(2, 0)
    block_arrived(1, 1)
    block_arrived(3, 0)
    share_pieces()
    block_arrived(2, 1)
    block_arrived(4, 0)
    block_arrived(3, 1)
    block_arrived(5, 0)
    hand_pieces()
    block_arrived(4, 1)
    block_arrived(6, 0)
    block_arrived(5, 1)
    take_filters()
    multiply(2, (0, 8))
    multiply(0, (0, 16))
    multiply_halo(1)
    biases.wait_recv()
    block_arrived(6, 1)
    multiply(2, (8, 16))

    column = lax.broadcasted_iota(jnp.int32, (64, 512), 1)
    offset = jnp.concatenate([bias_own[:, 0:1], bias_in[:, 0:1]], axis=0)
    offset = jnp.where(z_lo == 0, offset, jnp.zeros_like(offset))

    def tap(a, b):
        return 3 * a + b + z_lo * (8 - 2 * (3 * a + b))

    def finish(r, terms, side=None):
        sums = [sum(products[q, tap(a, b)] for q, a in terms) for b in range(3)]
        if side is not None:
            sums = [s + halo_products[side, b + z_lo * (2 - 2 * b)] for b, s in enumerate(sums)]
        left, mid, right = sums
        left = jnp.where(column == 0, 0.0, pltpu.roll(left, 1, 1))
        right = jnp.where(column == 511, 0.0, pltpu.roll(right, 511, 1))
        total = (left + mid + right + offset).astype(BF16)
        low, high = total[0:32], total[32:64]
        for side, own in ((0, features), (1, image_grad)):
            @pl.when(z_lo == side)
            def _():
                own[r] = high if side else low
                staged[r] = low if side else high
                remote(staged.at[r], own.at[r], out_send.at[r], out_recv.at[r], partner).start()
        return remote(staged.at[r], features.at[r], out_send.at[r], out_recv.at[r], partner)

    outgoing = [finish(r, [(POSITION[r + a - 1], a) for a in range(3)]) for r in (1, 2)]
    outgoing.append(finish(3 - 3 * core, [(1 - core, 1), (3 - core, 2 * core)], 1))

    @pl.when(outer_ok)
    def _():
        multiply_halo(0)

    @pl.when(jnp.logical_not(outer_ok))
    def _():
        halo_products[0] = jnp.zeros((3, 64, 512), F32)

    outgoing.append(finish(3 * core, [(core, 1), (2 + core, 2 - 2 * core)], 0))

    for copy in started:
        copy.wait_send()
    for slot in range(16):
        remote(give.at[0], halo.at[1, slot], halo_send.at[1, slot], halo_recv.at[1, slot], twin).wait_send()

    @pl.when(outer_ok)
    def _():
        for slot in range(16):
            remote(give.at[0], halo.at[0, slot], halo_send.at[0, slot], halo_recv.at[0, slot], twin).wait_send()

    @pl.when(sends_filters)
    def _():
        for d in range(1, 8):
            remote(packed.at[0], pieces.at[:, 0], piece_send.at[d], piece_recv.at[0], partner).wait_send()

        @pl.when(z_lo == 1)
        def _():
            remote(packed.at[0], pieces.at[:, 0], piece_send.at[0], piece_recv.at[0], partner).wait_send()

    @pl.when(gives_filters)
    def _():
        for j in range(2):
            from_partner(j).wait_send()

    @pl.when(z_lo == 0)
    def _():
        for m in range(2):
            for k in range(7):
                remote(pieces.at[:, 0], pieces.at[:, 0], share_send.at[m, k], piece_recv.at[0], partner).wait_send()

    @pl.when(takes_filters)
    def _():
        for j in range(2):
            for k in range(3):
                hand_on(j, k).wait_send()

    for copy in outgoing:
        copy.wait()


def channels_first(features, image_grad, features_out, image_grad_out, turned, sem):
    copies = []
    for k, (source, out) in enumerate(((features, features_out), (image_grad, image_grad_out))):
        turned[k] = jnp.transpose(source[...], (1, 0, 2))
        copies.append(pltpu.make_async_copy(turned.at[k], out, sem.at[k]))
        copies[-1].start()
    for copy in copies:
        copy.wait()


def per_device(image, filters, bias, upstream):
    filt = jnp.transpose(filters, (0, 2, 1))
    block = jax.ShapeDtypeStruct((4, 32, 512), BF16)
    dma = pltpu.SemaphoreType.DMA
    features, image_grad = pl.pallas_call(
        kernel,
        out_shape=(block, block),
        in_specs=[pl.BlockSpec(memory_space=pltpu.HBM)] * 4,
        out_specs=(pl.BlockSpec(memory_space=pltpu.VMEM),) * 2,
        scratch_shapes=[
            pltpu.VMEM((2, 32, 4, 512), BF16),
            pltpu.VMEM((4, 32, 512), BF16),
            pltpu.VMEM((9, 32, 512), BF16),
            pltpu.VMEM((1, 32), BF16),
            pltpu.VMEM((4, 16, 32, 512), BF16),
            pltpu.VMEM((2, 16, 32, 512), BF16),
            pltpu.VMEM((10, 64, 512), BF16),
            pltpu.VMEM((8, 5, 32, 128), BF16),
            pltpu.VMEM((5, 16, 32, 128), BF16),
            pltpu.VMEM((4, 9, 64, 512), F32),
            pltpu.VMEM((2, 3, 64, 512), F32),
            pltpu.VMEM((32, 128), F32),
            pltpu.VMEM((32, 128), F32),
            pltpu.VMEM((4, 32, 512), BF16),
            dma((4,)), dma((2, 7, 2)), dma((2, 7, 2)), dma((3,)), dma((3,)), dma((2, 16)), dma((2, 16)),
            dma((2,)), dma((4,)), dma((2, 3)), dma((8,)), dma((16,)), dma((2, 7)),
            dma((4,)), dma((4,)),
        ],
        compiler_params=pltpu.CompilerParams(
            collective_id=0, has_side_effects=True, vmem_limit_bytes=40 << 20),
        name="conv_both",
    )(*(pltpu.with_memory_space_constraint(value, pltpu.HBM)
        for value in (image, upstream, filt, bias.reshape(1, 32))))
    result = jax.ShapeDtypeStruct((32, 4, 512), BF16)
    return pl.pallas_call(
        channels_first,
        out_shape=(result, result),
        in_specs=[pl.BlockSpec(memory_space=pltpu.VMEM)] * 2,
        out_specs=(pl.BlockSpec(memory_space=pltpu.HBM),) * 2,
        scratch_shapes=[pltpu.VMEM((2, 32, 4, 512), BF16), dma((2,))],
        compiler_params=pltpu.CompilerParams(vmem_limit_bytes=8 << 20),
        name="channels_first",
    )(features, image_grad)


def solution(mesh):
    return jax.shard_map(
        per_device,
        mesh=mesh,
        in_specs=(
            P("chan", "band", None),
            P(None, None, "chan"),
            P("chan"),
            P("chan", "band", None),
        ),
        out_specs=(P("chan", "band", None), P("chan", "band", None)),
        check_vma=False,
    )
```

```python
import jax
import jax.numpy as jnp
from jax import lax
from jax.experimental import pallas as pl
from jax.experimental.pallas import tpu as pltpu
from jax.sharding import PartitionSpec as P

MESH = pl.DeviceIdType.MESH
BF16, F32 = jnp.bfloat16, jnp.float32


POSITION = (0, 2, 3, 1)


def kernel(image, upstream, filters, bias_row, features, image_grad, natural, give, filt, bias,
           gathered, halo, weights, packed, pieces, products, halo_products, bias_own, bias_in,
           staged, load_sem, ring_send, ring_recv, pair_send, pair_recv, halo_send, halo_recv,
           filter_send, filter_recv, relay_send, piece_send, piece_recv, share_send,
           out_send, out_recv):
    band, chan = lax.axis_index("band"), lax.axis_index("chan")
    core, x, z_hi = band % 2, (band // 2) % 4, band // 8
    y, z_lo = chan // 2, chan % 2
    partner_chan = chan + 1 - 2 * z_lo
    partner = {"band": band, "chan": partner_chan}
    ring_next = ({"band": band, "chan": (chan + 2) % 16}, {"band": band, "chan": (chan + 14) % 16})
    twin = {"band": band + 1 - 2 * core, "chan": chan}
    outer_ok = ((core == 0) & (band > 0)) | ((core == 1) & (band < 31))
    outer = {"band": (band + 31 + 2 * core) % 32, "chan": chan}
    sends_filters = (core == z_lo) & (x == y % 4)

    def slot_at(owner, place):
        return (owner + 16 - 4 * (((place + 7) // 2) % 4)) % 16

    def slot_of(owner):
        return slot_at(owner, y)

    def remote(src, dst, send, recv, where):
        return pltpu.make_async_remote_copy(
            src_ref=src, dst_ref=dst, send_sem=send, recv_sem=recv,
            device_id=where, device_id_type=MESH)

    loads = [pltpu.make_async_copy(filters, filt, load_sem.at[2]),
             pltpu.make_async_copy(bias_row, bias, load_sem.at[3])]
    keeping = [pltpu.make_async_copy(image, natural.at[z_lo], load_sem.at[0]),
               pltpu.make_async_copy(upstream, natural.at[1 - z_lo], load_sem.at[1])]
    for copy in keeping + loads:
        copy.start()

    barrier = pltpu.get_barrier_semaphore()

    def greet(where):
        pl.semaphore_signal(barrier, inc=1, device_id=where, device_id_type=MESH)

    def other_x(k):
        return {"band": z_hi * 8 + ((x + k) % 4) * 2 + core, "chan": chan}

    inner = (x == 1) | (x == 2)
    gives_filters, takes_filters = (z_lo == 0) & inner, (z_lo == 1) & inner

    def at_x(place, unit):
        return {"band": z_hi * 8 + place * 2 + unit, "chan": chan}

    for where in (partner, *ring_next, twin):
        greet(where)

    @pl.when(outer_ok)
    def _():
        greet(outer)

    @pl.when(z_lo == core)
    def _():
        for m in range(2):
            source = 2 * (x + 4 * m) + core

            @pl.when(source != chan)
            def _():
                greet({"band": band, "chan": source})

    @pl.when(z_lo == 0)
    def _():
        for k in range(1, 4):
            greet(other_x(k))

    @pl.when((z_lo == 1) & jnp.logical_not(inner))
    def _():
        for unit in range(2):
            greet(at_x(1 + x // 2, unit))

    own_slot = slot_of(chan)
    for copy in keeping:
        copy.wait()
    for row in range(4):
        gathered[POSITION[row], own_slot] = natural[0, :, row, :]
        give[POSITION[row]] = natural[1, :, row, :]

    targets = 4 + jnp.where(outer_ok, 1, 0) + jnp.where(z_lo == 0, 3, 0)
    targets = targets + jnp.where(sends_filters, 7, 0) + jnp.where(takes_filters, 2, 0)
    pl.semaphore_wait(barrier, targets)

    def rows(part):
        return slice(2 * part, 2 * part + 2)

    def ring(direction, hop, part, owner, src):
        place = (y + 1) % 8 if direction == 0 else (y + 7) % 8
        return remote(src, gathered.at[rows(part), slot_at(owner, place)],
                      ring_send.at[direction, hop, part], ring_recv.at[direction, hop, part],
                      ring_next[direction])

    def own_block(part, owner):
        return gathered.at[rows(part), slot_of(owner)]

    def halo_copy(side, owner, src):
        slot = slot_of(owner)
        return remote(src, halo.at[side, slot], halo_send.at[side, slot],
                      halo_recv.at[side, slot], twin if side else outer)

    def send_halo(owner):
        slot = slot_of(owner)

        @pl.when(outer_ok)
        def _():
            halo_copy(0, owner, gathered.at[core, slot]).start()

        halo_copy(1, owner, gathered.at[1 - core, slot]).start()

    started = []

    def start(copy):
        copy.start()
        started.append(copy)

    pairs = [remote(give.at[rows(part)], gathered.at[rows(part), own_slot],
                    pair_send.at[part], pair_recv.at[part], partner) for part in range(2)]
    for part in range(2):
        start(pairs[part])
        for direction in range(2):
            start(ring(direction, 0, part, chan, own_block(part, chan)))
    send_halo(chan)
    turn = ((y + 7) // 2) % 4

    def lanes(j):
        return pl.ds(pl.multiple_of(128 * ((j + turn) % 4), 128), 128)

    def from_partner(j):
        column = pl.ds(pl.multiple_of(128 * (2 * core + j), 128), 128)
        return remote(filt.at[:, :, lanes(2 * core + j)], weights.at[0:9, 0:32, column],
                      filter_send.at[j], filter_recv.at[2 * core + j], partner)

    def hand_on(j, k):
        column = pl.ds(pl.multiple_of(128 * (2 * core + j), 128), 128)
        place = jnp.where(x == 1, 0, 3)
        return remote(weights.at[0:9, 0:32, column], weights.at[0:9, 0:32, column],
                      relay_send.at[j, k], filter_recv.at[2 * core + j],
                      (twin, at_x(place, 0), at_x(place, 1))[k])

    def filters_wait(j, unit):
        remote(filt.at[:, :, 0:128], weights.at[0:9, 0:32, 0:128],
               relay_send.at[j, 0], filter_recv.at[2 * unit + j], twin).wait_recv()

    biases = remote(bias_own, bias_in, pair_send.at[2], pair_recv.at[2], partner)

    def prepare():
        for copy in loads:
            copy.wait()

        @pl.when(sends_filters)
        def _():
            lane = lax.broadcasted_iota(jnp.int32, (32, 128), 1)
            for q in range(4):
                for j in range(5):
                    a = filt[2 * j, :, 128 * q : 128 * q + 128].astype(F32)
                    b = filt[2 * j + 1, :, 128 * q : 128 * q + 128].astype(F32) if j < 4 else a
                    packed[2 * q, j] = jnp.where(lane < 64, a, pltpu.roll(b, 64, 1)).astype(BF16)
                    packed[2 * q + 1, j] = jnp.where(lane < 64, pltpu.roll(a, 64, 1), b).astype(BF16)
            for d in range(1, 8):
                place = (y + d) % 8
                slot = slot_at(chan, place)
                remote(packed.at[place], pieces.at[:, slot], piece_send.at[d],
                       piece_recv.at[slot], {"band": band, "chan": 2 * place + z_lo}).start()
            slot = slot_of(chan)

            @pl.when(z_lo == 0)
            def _():
                pltpu.make_async_copy(packed.at[y], pieces.at[:, slot], piece_recv.at[slot]).start()

            @pl.when(z_lo == 1)
            def _():
                remote(packed.at[y], pieces.at[:, slot], piece_send.at[0],
                       piece_recv.at[slot], partner).start()

        diagonal = (lax.broadcasted_iota(jnp.int32, (32, 32), 0)
                    == lax.broadcasted_iota(jnp.int32, (32, 32), 1))
        spread = jnp.where(diagonal, jnp.broadcast_to(bias[...].astype(F32), (32, 32)), 0.0)
        bias_own[...] = jnp.broadcast_to(jnp.sum(spread, axis=1, keepdims=True), (32, 128))
        start(biases)

        @pl.when(z_lo == 1)
        def _():
            for j in range(4):
                weights[0:9, 32:64, 128 * j : 128 * j + 128] = filt[:, :, lanes(j)]

        @pl.when(gives_filters)
        def _():
            for j in range(2):
                from_partner(j).start()

    def pair_arrived(part):
        pairs[part].wait_recv()
        for direction in range(2):
            start(ring(direction, 1, part, partner_chan, own_block(part, partner_chan)))
        if part == 0:
            send_halo(partner_chan)

    def piece_wait(owner):
        slot = slot_of(owner)
        remote(packed.at[0], pieces.at[:, slot], piece_send.at[0], piece_recv.at[slot], partner).wait_recv()

    def owner_of(direction, hop):
        away = hop // 2 + 1
        base = (chan + 16 - 2 * away) % 16 if direction == 0 else (chan + 2 * away) % 16
        swap = hop % 2 == 1 if hop < 6 else direction == 1
        return base + 1 - 2 * z_lo if swap else base

    def multiply(first, slots):
        lanes_of = slice(32 * slots[0], 32 * slots[1])
        depth = 32 * (slots[1] - slots[0])
        lhs = weights[0:9, :, lanes_of].reshape(576, depth)

        def body(q, carry):
            for n in range(2):
                columns = slice(256 * n, 256 * n + 256)
                rhs = gathered[q, slots[0] : slots[1], :, columns].reshape(depth, 256)
                result = jnp.dot(lhs, rhs, preferred_element_type=F32).reshape(9, 64, 256)
                if slots[0]:
                    result = products[q, :, :, columns] + result
                products[q, :, :, columns] = result
            return carry

        lax.fori_loop(first, first + 2, body, 0)

    def multiply_halo(side):
        for slot in range(16):
            remote(give.at[0], halo.at[side, slot], halo_send.at[side, slot],
                   halo_recv.at[side, slot], twin).wait_recv()
        turned = (core + z_lo + side) % 2
        lhs = weights[pl.ds(6 * turned, 3)].reshape(192, 512)
        rhs = halo[side].reshape(512, 512)
        halo_products[side] = jnp.dot(lhs, rhs, preferred_element_type=F32).reshape(3, 64, 512)

    def block_arrived(hop, part):
        for direction in range(2):
            owner = owner_of(direction, hop)
            ring(direction, hop, part, owner, give.at[rows(part)]).wait_recv()
            onward = hop + 2 if hop < 4 or (hop == 4 and direction == 0) else None
            if hop == 5 and direction == 1:
                onward = 6
            if onward is not None:
                start(ring(direction, onward, part, owner, own_block(part, owner)))
            if part == 0:
                send_halo(owner)

    def cross(m):
        owner = 2 * (x + 4 * m) + core
        slot = slot_of(owner)
        return owner, remote(pieces.at[:, slot], pieces.at[:, slot], share_send.at[m, 0],
                             piece_recv.at[slot], partner)

    def cross_pieces(ending):
        @pl.when((z_lo == 1) & (core == 1))
        def _():
            for m in range(2):
                owner, copy = cross(m)

                @pl.when(owner != chan)
                def _():
                    if ending:
                        copy.wait_send()
                    else:
                        piece_wait(owner)
                        copy.start()

    def share_pieces():
        @pl.when(z_lo == 0)
        def _():
            for m in range(2):
                owner = 2 * (x + 4 * m) + core
                piece_wait(owner)
                slot = slot_of(owner)
                for k in range(4):
                    remote(pieces.at[:, slot], pieces.at[:, slot], share_send.at[m, k],
                           piece_recv.at[slot], other_x(k) if k else twin).start()

        @pl.when(takes_filters)
        def _():
            for j in range(2):
                filters_wait(j, core)
                for k in range(3):
                    hand_on(j, k).start()

    def hand_pieces():
        @pl.when(z_lo == 0)
        def _():
            for k in range(1, 4):
                for m in range(2):
                    owner = 2 * ((x + k) % 4 + 4 * m) + core
                    piece_wait(owner)
                    slot = slot_of(owner)
                    remote(pieces.at[:, slot], pieces.at[:, slot], share_send.at[m, 3 + k],
                           piece_recv.at[slot], twin).start()

    def take_filters():
        @pl.when(z_lo == 0)
        def _():
            for k in range(4):
                for m in range(2):
                    piece_wait(2 * (k + 4 * m) + 1 - core)
            for j in range(5):
                weights[2 * j : 2 * j + 2] = pieces[j].reshape(512, 128).T.reshape(2, 64, 512)

        @pl.when(z_lo == 1)
        def _():
            for j in range(2):
                filters_wait(j, 1 - core)

            @pl.when(jnp.logical_not(inner))
            def _():
                for j in range(2):
                    filters_wait(j, core)

    prepare()
    pair_arrived(0)
    block_arrived(0, 0)
    pair_arrived(1)
    block_arrived(1, 0)
    block_arrived(0, 1)
    cross_pieces(False)
    block_arrived(2, 0)
    block_arrived(1, 1)
    block_arrived(3, 0)
    share_pieces()
    block_arrived(2, 1)
    block_arrived(4, 0)
    block_arrived(3, 1)
    block_arrived(5, 0)
    hand_pieces()
    block_arrived(4, 1)
    block_arrived(6, 0)
    block_arrived(5, 1)
    take_filters()
    multiply(2, (0, 8))
    multiply(0, (0, 16))
    multiply_halo(1)
    biases.wait_recv()
    block_arrived(6, 1)
    multiply(2, (8, 16))

    column = lax.broadcasted_iota(jnp.int32, (64, 512), 1)
    offset = jnp.concatenate([bias_own[:, 0:1], bias_in[:, 0:1]], axis=0)
    offset = jnp.where(z_lo == 0, offset, jnp.zeros_like(offset))

    def tap(a, b):
        return 3 * a + b + z_lo * (8 - 2 * (3 * a + b))

    def finish(r, terms, side=None):
        sums = [sum(products[q, tap(a, b)] for q, a in terms) for b in range(3)]
        if side is not None:
            sums = [s + halo_products[side, b + z_lo * (2 - 2 * b)] for b, s in enumerate(sums)]
        left, mid, right = sums
        left = jnp.where(column == 0, 0.0, pltpu.roll(left, 1, 1))
        right = jnp.where(column == 511, 0.0, pltpu.roll(right, 511, 1))
        total = (left + mid + right + offset).astype(BF16)
        low, high = total[0:32], total[32:64]
        for side, own in ((0, features), (1, image_grad)):
            @pl.when(z_lo == side)
            def _():
                own[r] = high if side else low
                staged[r] = low if side else high
                remote(staged.at[r], own.at[r], out_send.at[r], out_recv.at[r], partner).start()
        return remote(staged.at[r], features.at[r], out_send.at[r], out_recv.at[r], partner)

    outgoing = [finish(r, [(POSITION[r + a - 1], a) for a in range(3)]) for r in (1, 2)]
    outgoing.append(finish(3 - 3 * core, [(1 - core, 1), (3 - core, 2 * core)], 1))

    @pl.when(outer_ok)
    def _():
        multiply_halo(0)

    @pl.when(jnp.logical_not(outer_ok))
    def _():
        halo_products[0] = jnp.zeros((3, 64, 512), F32)

    outgoing.append(finish(3 * core, [(core, 1), (2 + core, 2 - 2 * core)], 0))

    for copy in started:
        copy.wait_send()
    for slot in range(16):
        remote(give.at[0], halo.at[1, slot], halo_send.at[1, slot], halo_recv.at[1, slot], twin).wait_send()

    @pl.when(outer_ok)
    def _():
        for slot in range(16):
            remote(give.at[0], halo.at[0, slot], halo_send.at[0, slot], halo_recv.at[0, slot], twin).wait_send()

    cross_pieces(True)

    @pl.when(sends_filters)
    def _():
        for d in range(1, 8):
            remote(packed.at[0], pieces.at[:, 0], piece_send.at[d], piece_recv.at[0], partner).wait_send()

        @pl.when(z_lo == 1)
        def _():
            remote(packed.at[0], pieces.at[:, 0], piece_send.at[0], piece_recv.at[0], partner).wait_send()

    @pl.when(gives_filters)
    def _():
        for j in range(2):
            from_partner(j).wait_send()

    @pl.when(z_lo == 0)
    def _():
        for m in range(2):
            for k in range(7):
                remote(pieces.at[:, 0], pieces.at[:, 0], share_send.at[m, k], piece_recv.at[0], partner).wait_send()

    @pl.when(takes_filters)
    def _():
        for j in range(2):
            for k in range(3):
                hand_on(j, k).wait_send()

    for copy in outgoing:
        copy.wait()


def channels_first(features, image_grad, features_out, image_grad_out, turned, sem):
    copies = []
    for k, (source, out) in enumerate(((features, features_out), (image_grad, image_grad_out))):
        turned[k] = jnp.transpose(source[...], (1, 0, 2))
        copies.append(pltpu.make_async_copy(turned.at[k], out, sem.at[k]))
        copies[-1].start()
    for copy in copies:
        copy.wait()


def per_device(image, filters, bias, upstream):
    filt = jnp.transpose(filters, (0, 2, 1))
    block = jax.ShapeDtypeStruct((4, 32, 512), BF16)
    dma = pltpu.SemaphoreType.DMA
    features, image_grad = pl.pallas_call(
        kernel,
        out_shape=(block, block),
        in_specs=[pl.BlockSpec(memory_space=pltpu.HBM)] * 4,
        out_specs=(pl.BlockSpec(memory_space=pltpu.VMEM),) * 2,
        scratch_shapes=[
            pltpu.VMEM((2, 32, 4, 512), BF16),
            pltpu.VMEM((4, 32, 512), BF16),
            pltpu.VMEM((9, 32, 512), BF16),
            pltpu.VMEM((1, 32), BF16),
            pltpu.VMEM((4, 16, 32, 512), BF16),
            pltpu.VMEM((2, 16, 32, 512), BF16),
            pltpu.VMEM((10, 64, 512), BF16),
            pltpu.VMEM((8, 5, 32, 128), BF16),
            pltpu.VMEM((5, 16, 32, 128), BF16),
            pltpu.VMEM((4, 9, 64, 512), F32),
            pltpu.VMEM((2, 3, 64, 512), F32),
            pltpu.VMEM((32, 128), F32),
            pltpu.VMEM((32, 128), F32),
            pltpu.VMEM((4, 32, 512), BF16),
            dma((4,)), dma((2, 7, 2)), dma((2, 7, 2)), dma((3,)), dma((3,)), dma((2, 16)), dma((2, 16)),
            dma((2,)), dma((4,)), dma((2, 3)), dma((8,)), dma((16,)), dma((2, 7)),
            dma((4,)), dma((4,)),
        ],
        compiler_params=pltpu.CompilerParams(
            collective_id=0, has_side_effects=True, vmem_limit_bytes=40 << 20),
        name="conv_both",
    )(*(pltpu.with_memory_space_constraint(value, pltpu.HBM)
        for value in (image, upstream, filt, bias.reshape(1, 32))))
    result = jax.ShapeDtypeStruct((32, 4, 512), BF16)
    return pl.pallas_call(
        channels_first,
        out_shape=(result, result),
        in_specs=[pl.BlockSpec(memory_space=pltpu.VMEM)] * 2,
        out_specs=(pl.BlockSpec(memory_space=pltpu.HBM),) * 2,
        scratch_shapes=[pltpu.VMEM((2, 32, 4, 512), BF16), dma((2,))],
        compiler_params=pltpu.CompilerParams(vmem_limit_bytes=8 << 20),
        name="channels_first",
    )(features, image_grad)


def solution(mesh):
    return jax.shard_map(
        per_device,
        mesh=mesh,
        in_specs=(
            P("chan", "band", None),
            P(None, None, "chan"),
            P("chan"),
            P("chan", "band", None),
        ),
        out_specs=(P("chan", "band", None), P("chan", "band", None)),
        check_vma=False,
    )
```

```python
import jax
import jax.numpy as jnp
from jax import lax
from jax.experimental import pallas as pl
from jax.experimental.pallas import tpu as pltpu
from jax.sharding import PartitionSpec as P

MESH = pl.DeviceIdType.MESH
BF16, F32 = jnp.bfloat16, jnp.float32


POSITION = (0, 2, 3, 1)


def kernel(image, upstream, filters, bias_row, features, image_grad, natural, give, filt, bias,
           gathered, halo, weights, packed, pieces, products, halo_products, bias_own, bias_in,
           staged, load_sem, ring_send, ring_recv, pair_send, pair_recv, halo_send, halo_recv,
           filter_send, filter_recv, relay_send, piece_send, piece_recv, share_send,
           out_send, out_recv):
    band, chan = lax.axis_index("band"), lax.axis_index("chan")
    core, x, z_hi = band % 2, (band // 2) % 4, band // 8
    y, z_lo = chan // 2, chan % 2
    partner_chan = chan + 1 - 2 * z_lo
    partner = {"band": band, "chan": partner_chan}
    ring_next = ({"band": band, "chan": (chan + 2) % 16}, {"band": band, "chan": (chan + 14) % 16})
    twin = {"band": band + 1 - 2 * core, "chan": chan}
    outer_ok = ((core == 0) & (band > 0)) | ((core == 1) & (band < 31))
    outer = {"band": (band + 31 + 2 * core) % 32, "chan": chan}
    sends_filters = (core == z_lo) & (x == y % 4)

    def slot_at(owner, place):
        return (owner + 16 - 4 * (((place + 7) // 2) % 4)) % 16

    def slot_of(owner):
        return slot_at(owner, y)

    def remote(src, dst, send, recv, where):
        return pltpu.make_async_remote_copy(
            src_ref=src, dst_ref=dst, send_sem=send, recv_sem=recv,
            device_id=where, device_id_type=MESH)

    loads = [pltpu.make_async_copy(filters, filt, load_sem.at[2]),
             pltpu.make_async_copy(bias_row, bias, load_sem.at[3])]
    keeping = [pltpu.make_async_copy(image, natural.at[z_lo], load_sem.at[0]),
               pltpu.make_async_copy(upstream, natural.at[1 - z_lo], load_sem.at[1])]
    barrier = pltpu.get_barrier_semaphore()

    def greet(where):
        pl.semaphore_signal(barrier, inc=1, device_id=where, device_id_type=MESH)

    def other_x(k):
        return {"band": z_hi * 8 + ((x + k) % 4) * 2 + core, "chan": chan}

    inner = (x == 1) | (x == 2)
    gives_filters, takes_filters = (z_lo == 0) & inner, (z_lo == 1) & inner

    def at_x(place, unit):
        return {"band": z_hi * 8 + place * 2 + unit, "chan": chan}

    for where in (*ring_next, partner):
        greet(where)
    for copy in keeping + loads:
        copy.start()
    greet(twin)

    @pl.when(outer_ok)
    def _():
        greet(outer)

    @pl.when(z_lo == core)
    def _():
        for m in range(2):
            source = 2 * (x + 4 * m) + core

            @pl.when(source != chan)
            def _():
                greet({"band": band, "chan": source})

    @pl.when(z_lo == 0)
    def _():
        for k in range(1, 4):
            greet(other_x(k))

    @pl.when((z_lo == 1) & jnp.logical_not(inner))
    def _():
        for unit in range(2):
            greet(at_x(1 + x // 2, unit))

    own_slot = slot_of(chan)
    for copy in keeping:
        copy.wait()
    for row in range(4):
        gathered[POSITION[row], own_slot] = natural[0, :, row, :]
        give[POSITION[row]] = natural[1, :, row, :]

    targets = 4 + jnp.where(outer_ok, 1, 0) + jnp.where(z_lo == 0, 3, 0)
    targets = targets + jnp.where(sends_filters, 7, 0) + jnp.where(takes_filters, 2, 0)
    pl.semaphore_wait(barrier, targets)

    def rows(part):
        return slice(2 * part, 2 * part + 2)

    def ring(direction, hop, part, owner, src):
        place = (y + 1) % 8 if direction == 0 else (y + 7) % 8
        return remote(src, gathered.at[rows(part), slot_at(owner, place)],
                      ring_send.at[direction, hop, part], ring_recv.at[direction, hop, part],
                      ring_next[direction])

    def own_block(part, owner):
        return gathered.at[rows(part), slot_of(owner)]

    def halo_copy(side, owner, src):
        slot = slot_of(owner)
        return remote(src, halo.at[side, slot], halo_send.at[side, slot],
                      halo_recv.at[side, slot], twin if side else outer)

    def send_halo(owner):
        slot = slot_of(owner)

        @pl.when(outer_ok)
        def _():
            halo_copy(0, owner, gathered.at[core, slot]).start()

        halo_copy(1, owner, gathered.at[1 - core, slot]).start()

    started = []

    def start(copy):
        copy.start()
        started.append(copy)

    pairs = [remote(give.at[rows(part)], gathered.at[rows(part), own_slot],
                    pair_send.at[part], pair_recv.at[part], partner) for part in range(2)]
    for part in range(2):
        start(pairs[part])
        for direction in range(2):
            start(ring(direction, 0, part, chan, own_block(part, chan)))
    send_halo(chan)
    turn = ((y + 7) // 2) % 4

    def lanes(j):
        return pl.ds(pl.multiple_of(128 * ((j + turn) % 4), 128), 128)

    def from_partner(j):
        column = pl.ds(pl.multiple_of(128 * (2 * core + j), 128), 128)
        return remote(filt.at[:, :, lanes(2 * core + j)], weights.at[0:9, 0:32, column],
                      filter_send.at[j], filter_recv.at[2 * core + j], partner)

    def hand_on(j, k):
        column = pl.ds(pl.multiple_of(128 * (2 * core + j), 128), 128)
        place = jnp.where(x == 1, 0, 3)
        return remote(weights.at[0:9, 0:32, column], weights.at[0:9, 0:32, column],
                      relay_send.at[j, k], filter_recv.at[2 * core + j],
                      (twin, at_x(place, 0), at_x(place, 1))[k])

    def filters_wait(j, unit):
        remote(filt.at[:, :, 0:128], weights.at[0:9, 0:32, 0:128],
               relay_send.at[j, 0], filter_recv.at[2 * unit + j], twin).wait_recv()

    biases = remote(bias_own, bias_in, pair_send.at[2], pair_recv.at[2], partner)

    def prepare():
        for copy in loads:
            copy.wait()

        @pl.when(sends_filters)
        def _():
            lane = lax.broadcasted_iota(jnp.int32, (32, 128), 1)
            for q in range(4):
                for j in range(5):
                    a = filt[2 * j, :, 128 * q : 128 * q + 128].astype(F32)
                    b = filt[2 * j + 1, :, 128 * q : 128 * q + 128].astype(F32) if j < 4 else a
                    packed[2 * q, j] = jnp.where(lane < 64, a, pltpu.roll(b, 64, 1)).astype(BF16)
                    packed[2 * q + 1, j] = jnp.where(lane < 64, pltpu.roll(a, 64, 1), b).astype(BF16)
            for d in range(1, 8):
                place = (y + d) % 8
                slot = slot_at(chan, place)
                remote(packed.at[place], pieces.at[:, slot], piece_send.at[d],
                       piece_recv.at[slot], {"band": band, "chan": 2 * place + z_lo}).start()
            slot = slot_of(chan)

            @pl.when(z_lo == 0)
            def _():
                pltpu.make_async_copy(packed.at[y], pieces.at[:, slot], piece_recv.at[slot]).start()

            @pl.when(z_lo == 1)
            def _():
                remote(packed.at[y], pieces.at[:, slot], piece_send.at[0],
                       piece_recv.at[slot], partner).start()

        diagonal = (lax.broadcasted_iota(jnp.int32, (32, 32), 0)
                    == lax.broadcasted_iota(jnp.int32, (32, 32), 1))
        spread = jnp.where(diagonal, jnp.broadcast_to(bias[...].astype(F32), (32, 32)), 0.0)
        bias_own[...] = jnp.broadcast_to(jnp.sum(spread, axis=1, keepdims=True), (32, 128))
        start(biases)

        @pl.when(z_lo == 1)
        def _():
            for j in range(4):
                weights[0:9, 32:64, 128 * j : 128 * j + 128] = filt[:, :, lanes(j)]

        @pl.when(gives_filters)
        def _():
            for j in range(2):
                from_partner(j).start()

    def pair_arrived(part):
        pairs[part].wait_recv()
        for direction in range(2):
            start(ring(direction, 1, part, partner_chan, own_block(part, partner_chan)))
        if part == 0:
            send_halo(partner_chan)

    def piece_wait(owner):
        slot = slot_of(owner)
        remote(packed.at[0], pieces.at[:, slot], piece_send.at[0], piece_recv.at[slot], partner).wait_recv()

    def owner_of(direction, hop):
        away = hop // 2 + 1
        base = (chan + 16 - 2 * away) % 16 if direction == 0 else (chan + 2 * away) % 16
        swap = hop % 2 == 1 if hop < 6 else direction == 1
        return base + 1 - 2 * z_lo if swap else base

    def multiply(first, slots):
        lanes_of = slice(32 * slots[0], 32 * slots[1])
        depth = 32 * (slots[1] - slots[0])
        lhs = weights[0:9, :, lanes_of].reshape(576, depth)

        def body(q, carry):
            for n in range(2):
                columns = slice(256 * n, 256 * n + 256)
                rhs = gathered[q, slots[0] : slots[1], :, columns].reshape(depth, 256)
                result = jnp.dot(lhs, rhs, preferred_element_type=F32).reshape(9, 64, 256)
                if slots[0]:
                    result = products[q, :, :, columns] + result
                products[q, :, :, columns] = result
            return carry

        lax.fori_loop(first, first + 2, body, 0)

    def multiply_halo(side, slots=(0, 16)):
        for slot in range(*slots):
            remote(give.at[0], halo.at[side, slot], halo_send.at[side, slot],
                   halo_recv.at[side, slot], twin).wait_recv()
        turned = (core + z_lo + side) % 2
        depth = 32 * (slots[1] - slots[0])
        lhs = weights[pl.ds(6 * turned, 3), :, 32 * slots[0] : 32 * slots[1]].reshape(192, depth)
        rhs = halo[side, slots[0] : slots[1]].reshape(depth, 512)
        result = jnp.dot(lhs, rhs, preferred_element_type=F32).reshape(3, 64, 512)
        if slots[0]:
            result = halo_products[side] + result
        halo_products[side] = result

    def block_arrived(hop, part):
        for direction in range(2):
            owner = owner_of(direction, hop)
            ring(direction, hop, part, owner, give.at[rows(part)]).wait_recv()
            onward = hop + 2 if hop < 4 or (hop == 4 and direction == 0) else None
            if hop == 5 and direction == 1:
                onward = 6
            if onward is not None:
                start(ring(direction, onward, part, owner, own_block(part, owner)))
            if part == 0:
                send_halo(owner)

    def cross(m):
        owner = 2 * (x + 4 * m) + core
        slot = slot_of(owner)
        return owner, remote(pieces.at[:, slot], pieces.at[:, slot], share_send.at[m, 0],
                             piece_recv.at[slot], partner)

    def cross_pieces(ending):
        @pl.when((z_lo == 1) & (core == 1))
        def _():
            for m in range(2):
                owner, copy = cross(m)

                @pl.when(owner != chan)
                def _():
                    if ending:
                        copy.wait_send()
                    else:
                        piece_wait(owner)
                        copy.start()

    def share_pieces():
        @pl.when(z_lo == 0)
        def _():
            for m in range(2):
                owner = 2 * (x + 4 * m) + core
                piece_wait(owner)
                slot = slot_of(owner)
                for k in range(4):
                    remote(pieces.at[:, slot], pieces.at[:, slot], share_send.at[m, k],
                           piece_recv.at[slot], other_x(k) if k else twin).start()

        @pl.when(takes_filters)
        def _():
            for j in range(2):
                filters_wait(j, core)
                for k in range(3):
                    hand_on(j, k).start()

    def hand_pieces():
        @pl.when(z_lo == 0)
        def _():
            for k in range(1, 4):
                for m in range(2):
                    owner = 2 * ((x + k) % 4 + 4 * m) + core
                    piece_wait(owner)
                    slot = slot_of(owner)
                    remote(pieces.at[:, slot], pieces.at[:, slot], share_send.at[m, 3 + k],
                           piece_recv.at[slot], twin).start()

    def take_filters():
        @pl.when(z_lo == 0)
        def _():
            for k in range(4):
                for m in range(2):
                    piece_wait(2 * (k + 4 * m) + 1 - core)
            for j in range(5):
                weights[2 * j : 2 * j + 2] = pieces[j].reshape(512, 128).T.reshape(2, 64, 512)

        @pl.when(z_lo == 1)
        def _():
            for j in range(2):
                filters_wait(j, 1 - core)

            @pl.when(jnp.logical_not(inner))
            def _():
                for j in range(2):
                    filters_wait(j, core)

    prepare()
    pair_arrived(0)
    block_arrived(0, 0)
    pair_arrived(1)
    block_arrived(1, 0)
    block_arrived(0, 1)
    cross_pieces(False)
    block_arrived(2, 0)
    block_arrived(1, 1)
    block_arrived(3, 0)
    share_pieces()
    block_arrived(2, 1)
    block_arrived(4, 0)
    block_arrived(3, 1)
    block_arrived(5, 0)
    hand_pieces()
    block_arrived(4, 1)
    block_arrived(6, 0)
    block_arrived(5, 1)
    take_filters()
    multiply(2, (0, 8))
    multiply(0, (0, 16))
    multiply_halo(1)

    @pl.when(outer_ok)
    def _():
        multiply_halo(0, (0, 8))

    @pl.when(jnp.logical_not(outer_ok))
    def _():
        halo_products[0] = jnp.zeros((3, 64, 512), F32)

    biases.wait_recv()
    block_arrived(6, 1)
    multiply(2, (8, 16))

    column = lax.broadcasted_iota(jnp.int32, (64, 512), 1)
    offset = jnp.concatenate([bias_own[:, 0:1], bias_in[:, 0:1]], axis=0)
    offset = jnp.where(z_lo == 0, offset, jnp.zeros_like(offset))

    def tap(a, b):
        return 3 * a + b + z_lo * (8 - 2 * (3 * a + b))

    def finish(r, terms, side=None):
        sums = [sum(products[q, tap(a, b)] for q, a in terms) for b in range(3)]
        if side is not None:
            sums = [s + halo_products[side, b + z_lo * (2 - 2 * b)] for b, s in enumerate(sums)]
        left, mid, right = sums
        left = jnp.where(column == 0, 0.0, pltpu.roll(left, 1, 1))
        right = jnp.where(column == 511, 0.0, pltpu.roll(right, 511, 1))
        total = (left + mid + right + offset).astype(BF16)
        low, high = total[0:32], total[32:64]
        for side, own in ((0, features), (1, image_grad)):
            @pl.when(z_lo == side)
            def _():
                own[r] = high if side else low
                staged[r] = low if side else high
                remote(staged.at[r], own.at[r], out_send.at[r], out_recv.at[r], partner).start()
        return remote(staged.at[r], features.at[r], out_send.at[r], out_recv.at[r], partner)

    outgoing = [finish(r, [(POSITION[r + a - 1], a) for a in range(3)]) for r in (1, 2)]
    outgoing.append(finish(3 - 3 * core, [(1 - core, 1), (3 - core, 2 * core)], 1))

    @pl.when(outer_ok)
    def _():
        multiply_halo(0, (8, 16))

    outgoing.append(finish(3 * core, [(core, 1), (2 + core, 2 - 2 * core)], 0))

    for copy in started:
        copy.wait_send()
    for slot in range(16):
        remote(give.at[0], halo.at[1, slot], halo_send.at[1, slot], halo_recv.at[1, slot], twin).wait_send()

    @pl.when(outer_ok)
    def _():
        for slot in range(16):
            remote(give.at[0], halo.at[0, slot], halo_send.at[0, slot], halo_recv.at[0, slot], twin).wait_send()

    cross_pieces(True)

    @pl.when(sends_filters)
    def _():
        for d in range(1, 8):
            remote(packed.at[0], pieces.at[:, 0], piece_send.at[d], piece_recv.at[0], partner).wait_send()

        @pl.when(z_lo == 1)
        def _():
            remote(packed.at[0], pieces.at[:, 0], piece_send.at[0], piece_recv.at[0], partner).wait_send()

    @pl.when(gives_filters)
    def _():
        for j in range(2):
            from_partner(j).wait_send()

    @pl.when(z_lo == 0)
    def _():
        for m in range(2):
            for k in range(7):
                remote(pieces.at[:, 0], pieces.at[:, 0], share_send.at[m, k], piece_recv.at[0], partner).wait_send()

    @pl.when(takes_filters)
    def _():
        for j in range(2):
            for k in range(3):
                hand_on(j, k).wait_send()

    for copy in outgoing:
        copy.wait()


def channels_first(features, image_grad, features_out, image_grad_out, turned, sem):
    copies = []
    for k, (source, out) in enumerate(((features, features_out), (image_grad, image_grad_out))):
        turned[k] = jnp.transpose(source[...], (1, 0, 2))
        copies.append(pltpu.make_async_copy(turned.at[k], out, sem.at[k]))
        copies[-1].start()
    for copy in copies:
        copy.wait()


def per_device(image, filters, bias, upstream):
    filt = jnp.transpose(filters, (0, 2, 1))
    block = jax.ShapeDtypeStruct((4, 32, 512), BF16)
    dma = pltpu.SemaphoreType.DMA
    features, image_grad = pl.pallas_call(
        kernel,
        out_shape=(block, block),
        in_specs=[pl.BlockSpec(memory_space=pltpu.HBM)] * 4,
        out_specs=(pl.BlockSpec(memory_space=pltpu.VMEM),) * 2,
        scratch_shapes=[
            pltpu.VMEM((2, 32, 4, 512), BF16),
            pltpu.VMEM((4, 32, 512), BF16),
            pltpu.VMEM((9, 32, 512), BF16),
            pltpu.VMEM((1, 32), BF16),
            pltpu.VMEM((4, 16, 32, 512), BF16),
            pltpu.VMEM((2, 16, 32, 512), BF16),
            pltpu.VMEM((10, 64, 512), BF16),
            pltpu.VMEM((8, 5, 32, 128), BF16),
            pltpu.VMEM((5, 16, 32, 128), BF16),
            pltpu.VMEM((4, 9, 64, 512), F32),
            pltpu.VMEM((2, 3, 64, 512), F32),
            pltpu.VMEM((32, 128), F32),
            pltpu.VMEM((32, 128), F32),
            pltpu.VMEM((4, 32, 512), BF16),
            dma((4,)), dma((2, 7, 2)), dma((2, 7, 2)), dma((3,)), dma((3,)), dma((2, 16)), dma((2, 16)),
            dma((2,)), dma((4,)), dma((2, 3)), dma((8,)), dma((16,)), dma((2, 7)),
            dma((4,)), dma((4,)),
        ],
        compiler_params=pltpu.CompilerParams(
            collective_id=0, has_side_effects=True, vmem_limit_bytes=40 << 20),
        name="conv_both",
    )(*(pltpu.with_memory_space_constraint(value, pltpu.HBM)
        for value in (image, upstream, filt, bias.reshape(1, 32))))
    result = jax.ShapeDtypeStruct((32, 4, 512), BF16)
    return pl.pallas_call(
        channels_first,
        out_shape=(result, result),
        in_specs=[pl.BlockSpec(memory_space=pltpu.VMEM)] * 2,
        out_specs=(pl.BlockSpec(memory_space=pltpu.HBM),) * 2,
        scratch_shapes=[pltpu.VMEM((2, 32, 4, 512), BF16), dma((2,))],
        compiler_params=pltpu.CompilerParams(vmem_limit_bytes=8 << 20),
        name="channels_first",
    )(features, image_grad)


def solution(mesh):
    return jax.shard_map(
        per_device,
        mesh=mesh,
        in_specs=(
            P("chan", "band", None),
            P(None, None, "chan"),
            P("chan"),
            P("chan", "band", None),
        ),
        out_specs=(P("chan", "band", None), P("chan", "band", None)),
        check_vma=False,
    )
```
